512 devices in a mesh: light: 8 (over y), view: 64 (over z, x, core).
Axes of the slice: x: 4, y: 8, z: 8, core: 2. Of those that a mesh axis runs over, the one named last changes fastest.
Arguments:
- density: bfloat16 [32, 1024, 2048], P('light', 'view'), may hold values from 0 to 1
- occupied: int32 [8, 64, 16], P('light', 'view'), may hold values from 0 to 1, as said below
- view_sign: float32 [1], replicated, may hold values from -1 to 1, as said below
- transfer: float32 [4, 4], replicated, may hold values from -3 to 3
- absorb: float32 [3], replicated, may hold values from 0.5 to 20
- light_in: float32 [3, 1024, 2048], P(None, 'view'), may hold values from 1 to 2.5
Outputs:
- image: float32 [4, 65536], P(None, ('light', 'view'))
The draws below stay inside these ranges and needn't reach their ends.
Inputs may be any that keep to these rules, and one draw needn't show every extreme that they name: `occupied`: 0 or 1; the share of occupied bricks differs from device to device. `view_sign`: magnitude 0.5 or more; either sign.
All inputs are finite; a program needn't handle non-finite values.
Results may differ from the reference program's by a relative error of at most 0.0003.
Values may be sent and summed in bfloat16 or wider, within the bound.
No kernel may reach another device: no remote copies, remote signals or barrier semaphores. Data moves between devices by JAX's collectives and lax.ppermute only.
A program may use at most 64 MiB of HBM per device.

```python
import jax
import jax.numpy as jnp
from jax import lax

CX = 4
CY = 16
NZ = 2048
BRICK = 128
NX = 32
NY = 1024
BRICKS = 16


def draw_occupied(key, part):
    level_key, ticket_key = jax.random.split(jax.random.fold_in(key, 7))
    level = jax.random.randint(level_key, (NX // CX, NY // CY, 1), 1, 5)
    ticket = jax.random.randint(ticket_key, (NX // CX, NY // CY, BRICKS), 0, 4)
    return (ticket < level).astype(jnp.int32)


def draw_view_sign(key, part):
    magnitude = jax.random.uniform(jax.random.fold_in(key, 11), (1,), jnp.float32, 0.5, 1.0)
    return magnitude


def draw_density(key, part):
    high_key, low_key, noise_key = jax.random.split(jax.random.fold_in(key, 13), 3)
    column = jnp.arange(NZ, dtype=jnp.int32)
    noise = jax.random.uniform(noise_key, (NX, NY, NZ), jnp.float32, 0.0, 1.0)
    pattern = column // 2 % 2
    high = jax.random.uniform(high_key, (NX, 1, NZ), jnp.float32, 0.82, 1.0)
    low = jax.random.uniform(low_key, (NX, 1, NZ), jnp.float32, 0.0, 0.1)
    base = jnp.where(pattern[None, None, :] == 1, high, low)
    value = 0.85 * base + 0.15 * noise
    return value.astype(jnp.bfloat16)


def draw_transfer(key, part):
    keys = jax.random.split(jax.random.fold_in(key, 17), 5)
    first = jax.random.uniform(keys[0], (1,), jnp.float32, -3.0, -2.5)
    second = jax.random.uniform(keys[1], (1,), jnp.float32, 2.5, 3.0)
    third = jax.random.uniform(keys[2], (1,), jnp.float32, 1.5, 3.0)
    fourth = jax.random.uniform(keys[3], (1,), jnp.float32, 1.5, 3.0)
    extinction_row = jnp.concatenate([first, second, third, fourth])[None, :]
    colour_rows = jax.random.truncated_normal(keys[4], -3.0, 3.0, (3, 4), jnp.float32)
    return jnp.concatenate([extinction_row, colour_rows], axis=0)


def draw_absorb(key, part):
    keys = jax.random.split(jax.random.fold_in(key, 19), 4)
    bounds = ((0.5, 1.5), (3.0, 8.0), (12.0, 20.0))
    values = []
    for index in range(3):
        lower, upper = bounds[index]
        exponent = jax.random.uniform(keys[index], (1,), jnp.float32, jnp.log(lower), jnp.log(upper))
        values.append(jnp.clip(jnp.exp(exponent), lower, upper))
    stacked = jnp.concatenate(values)
    order = jax.random.permutation(keys[3], 3)
    return stacked[order]


def block_scale(stream_key, extent, cuts, least, top_value):
    factor_of, own = 1.0, jax.random.fold_in(stream_key, 6)
    for axis_at, shards_of in cuts:
        heights = jnp.exp(jax.random.uniform(jax.random.fold_in(own, axis_at), (shards_of,), jnp.float32, least / len(cuts), top_value / len(cuts)))
        factor_of = factor_of * jnp.repeat(heights, extent[axis_at] // shards_of).reshape([-1 if axis == axis_at else 1 for axis in range(len(extent))])
    return factor_of


def setup_inputs(seed: int = 0) -> dict:
    seeds = jax.random.split(jax.random.key(seed), 7)
    density = draw_density(jax.random.fold_in(seeds[6], 71), 0)
    occupied = draw_occupied(jax.random.fold_in(seeds[6], 71), 0)
    view_sign = draw_view_sign(jax.random.fold_in(seeds[6], 71), 0)
    transfer = draw_transfer(jax.random.fold_in(seeds[6], 71), 0)
    absorb = draw_absorb(jax.random.fold_in(seeds[6], 71), 0)
    light_in = jnp.clip(1.0 + 1.5 * jax.random.uniform(seeds[5], (3, NY, NZ), jnp.float32) ** block_scale(seeds[5], (3, NY, NZ), ((1, 64),), -0.2, 0.2), 1.0, 2.5)
    return {"density": density, "occupied": occupied, "view_sign": view_sign, "transfer": transfer, "absorb": absorb, "light_in": light_in}


def polynomial(coeffs, values):
    return coeffs[0] + values * (coeffs[1] + values * (coeffs[2] + values * coeffs[3]))

def blur_columns(field):
    widths = [(0, 0)] * (field.ndim - 1) + [(1, 1)]
    padded = jnp.pad(field, widths)
    return 0.25 * padded[..., :-2] + 0.5 * padded[..., 1:-1] + 0.25 * padded[..., 2:]

def composite_depth(emitted, opacity, facing_back):
    emitted = jnp.where(facing_back == 1, jnp.flip(emitted, 1), emitted)
    opacity = jnp.where(facing_back == 1, jnp.flip(opacity, 0), opacity)
    passing = 1.0 - opacity
    through = jnp.cumprod(passing, axis=0)
    before = jnp.concatenate([jnp.ones_like(passing[:1]), through[:-1]], axis=0)
    colour = lax.optimization_barrier(jnp.sum(before[None] * emitted, axis=1))
    return jnp.concatenate([colour, (1.0 - through[-1])[None]], axis=0)

def reference(density, occupied, view_sign, transfer, absorb, light_in):
    padded = jnp.pad(density, ((1, 1), (0, 0), (0, 0)))
    occupancy_all = jnp.repeat(occupied.astype(jnp.float32), BRICK, axis=2)
    occupancy_all = jnp.repeat(occupancy_all, CY, axis=1)
    facing_back = (view_sign[0] < 0.0).astype(jnp.int32)
    path_length = 2.0 / NY / jnp.abs(view_sign[0])

    def layer(light_front, layer_row):
        window = lax.dynamic_slice_in_dim(padded, layer_row, 3, 0).astype(jnp.float32)
        centre = window[1]
        occupancy = lax.dynamic_index_in_dim(occupancy_all, layer_row // CX, 0, keepdims=False)
        grad_x = 0.5 * (window[2] - window[0])
        bricked = centre.reshape(NY // CY, CY, NZ)
        side_y = jnp.pad(bricked, ((0, 0), (1, 1), (0, 0)), mode='edge')
        grad_y = (0.5 * (side_y[:, 2:, :] - side_y[:, :-2, :])).reshape(NY, NZ)
        side_z = jnp.pad(centre, ((0, 0), (1, 1)))
        grad_z = 0.5 * (side_z[:, 2:] - side_z[:, :-2])
        extinction = jax.nn.softplus(polynomial(transfer[0], centre)) * occupancy
        opacity = 1.0 - jnp.exp(-extinction * path_length)
        colour = jnp.stack([jax.nn.sigmoid(polynomial(transfer[channel], centre)) for channel in (1, 2, 3)], axis=0)
        facing = (0.8 * grad_x + 0.36 * grad_y + 0.48 * grad_z) * lax.rsqrt(1.0 + grad_x * grad_x + grad_y * grad_y + grad_z * grad_z)
        shading = 0.65 + 0.35 * facing
        transmit = jnp.exp(-absorb[:, None, None] * extinction[None] / NX)
        emitted = opacity[None] * colour * (0.2 + light_front * shading[None])
        pixel_row = composite_depth(emitted, opacity, facing_back)
        return (blur_columns(light_front * transmit), pixel_row)
    _, pixel_rows = lax.scan(layer, light_in, jnp.arange(NX, dtype=jnp.int32))
    return jnp.transpose(pixel_rows, (1, 0, 2)).reshape(4, NX * NZ)
```

```python
import jax
import jax.numpy as jnp
from jax import lax
from jax.experimental import pallas as pl
from jax.experimental.pallas import tpu as pltpu
from jax.sharding import PartitionSpec as P

S = 8
T = 256
H = 128
F32 = jnp.float32
BF16 = jnp.bfloat16
VMEM = pl.BlockSpec(memory_space=pltpu.VMEM)
SMEM = pl.BlockSpec(memory_space=pltpu.SMEM)


def halves(x):
    return x[..., :H], x[..., H:]


def lane_is(pos):
    return lax.broadcasted_iota(jnp.int32, (S, H), 1) == pos


def sub_is(pos):
    return lax.broadcasted_iota(jnp.int32, (S, H), 0) == pos


def previous(a, b):
    ra, rb = pltpu.roll(a, 1, a.ndim - 1), pltpu.roll(b, 1, a.ndim - 1)
    wrap = jnp.where(sub_is(0), 0.0, pltpu.roll(rb, 1, a.ndim - 2))
    first = lane_is(0)
    return jnp.where(first, wrap, ra), jnp.where(first, ra, rb)


def following(a, b):
    ra, rb = pltpu.roll(a, H - 1, a.ndim - 1), pltpu.roll(b, H - 1, a.ndim - 1)
    wrap = jnp.where(sub_is(S - 1), 0.0, pltpu.roll(ra, S - 1, a.ndim - 2))
    last = lane_is(H - 1)
    return jnp.where(last, rb, ra), jnp.where(last, wrap, rb)


def blur(a, b):
    pa, pb = previous(a, b)
    na, nb = following(a, b)
    return 0.25 * (pa + na) + 0.5 * a, 0.25 * (pb + nb) + 0.5 * b


def polynomial(coeffs, row, s):
    return coeffs[row, 0] + s * (coeffs[row, 1] + s * (coeffs[row, 2] + s * coeffs[row, 3]))


def softplus(x):
    u = jnp.exp(-jnp.abs(x))
    tail = jnp.where(u < 2.0**-8, u * (1.0 - u * (0.5 - u * (1.0 / 3.0))), jnp.log(1.0 + u))
    return jnp.maximum(x, 0.0) + tail


def brick_mask(occ_ref):
    sub = lax.broadcasted_iota(jnp.int32, (S, H), 0)
    out = []
    for h in range(2):
        occ = jnp.zeros((S, H), F32)
        for s in range(S):
            occ = jnp.where(sub == s, occ_ref[0, 0, 2 * s + h].astype(F32), occ)
        out.append(occ)
    return out


def prepare_kernel(dens_ref, occ_ref, light_ref, pos_ref, cells_ref, first_ref, last_ref, send_ref, rows_ref, tmp):
    layers, rows, _ = dens_ref.shape
    occ = brick_mask(occ_ref)
    mask = jnp.concatenate(occ, axis=1)[None] > 0.5
    for layer in range(layers):
        x = dens_ref[layer].astype(F32)
        for s in range(S):
            for h in range(2):
                column = (2 * s + h) * H
                tmp[pl.ds(h * rows * S + s, rows, stride=S), :] = x[:, column : column + H]
        y = jnp.concatenate([tmp[h * rows * S : (h + 1) * rows * S, :].reshape(rows, S, H) for h in range(2)], axis=2)
        raw = y.astype(BF16)
        cells_ref[layer] = raw
        if layer == 0:
            first_ref[...] = raw
        if layer == layers - 1:
            last_ref[...] = raw
        masked = jnp.where(mask, y, -1.0).astype(BF16)
        send_ref[:, layer] = masked.reshape(rows // 2, 2, S, T)
    start = 2 * pos_ref[0]
    for c in range(3):
        for r in range(2):
            for s in range(S):
                rows_ref[c, r, s : s + 1, :] = light_ref[c, pl.ds(start + r, 1), s * T : (s + 1) * T]


def propagate_kernel(recv_ref, rows_ref, transfer_ref, absorb_ref, send_ref):
    blocks, layers = recv_ref.shape[0], recv_ref.shape[1]
    scale = [-absorb_ref[c] / 32.0 for c in range(3)]

    def block(k, carry):
        front = list(carry)
        for c in range(3):
            a, b = front[c]
            send_ref[k, c, :, :, :H] = a.astype(BF16)
            send_ref[k, c, :, :, H:] = b.astype(BF16)
        for layer in range(layers):
            ext = []
            for d in halves(recv_ref[k, layer].astype(F32)):
                ext.append(jnp.where(d < 0.0, 0.0, softplus(polynomial(transfer_ref, 0, d))))
            for c in range(3):
                a, b = front[c]
                front[c] = blur(a * jnp.exp(scale[c] * ext[0]), b * jnp.exp(scale[c] * ext[1]))
        return tuple(front)

    init = tuple(halves(rows_ref[c]) for c in range(3))
    final = lax.fori_loop(0, blocks - 1, block, init)
    for c in range(3):
        send_ref[blocks - 1, c, :, :, :H] = final[c][0].astype(BF16)
        send_ref[blocks - 1, c, :, :, H:] = final[c][1].astype(BF16)


def local_kernel(cells_ref, low_ref, high_ref, occ_ref, sign_ref, transfer_ref, ext_ref, gain_ref, base_ref, *, total_y):
    layers, rows = cells_ref.shape[0], cells_ref.shape[1]
    occ = brick_mask(occ_ref)
    sign = sign_ref[0]
    back = sign < 0.0
    path = (2.0 / total_y) / jnp.abs(jnp.full((S, H), sign, F32))

    def load(layer, r):
        if layer < 0:
            v = low_ref[r]
        elif layer >= layers:
            v = high_ref[r]
        else:
            v = cells_ref[layer, r]
        return halves(v.astype(F32))

    def row(i, carry):
        r = jnp.where(back, rows - 1 - i, i)
        up = jnp.minimum(r + 1, rows - 1)
        down = jnp.maximum(r - 1, 0)
        column = [load(layer, r) for layer in range(-1, layers + 1)]
        new = []
        for layer in range(layers):
            through, base = carry[layer]
            d = column[layer + 1]
            dn, dp = load(layer, up), load(layer, down)
            zp, zn = previous(*d), following(*d)
            t_out, b_out = [], []
            for h in range(2):
                s = d[h]
                gx = 0.5 * (column[layer + 2][h] - column[layer][h])
                gy = 0.5 * (dn[h] - dp[h])
                gz = 0.5 * (zn[h] - zp[h])
                facing = (0.8 * gx + 0.36 * gy + 0.48 * gz) * lax.rsqrt(1.0 + gx * gx + gy * gy + gz * gz)
                shading = 0.65 + 0.35 * facing
                ext = softplus(polynomial(transfer_ref, 0, s)) * occ[h]
                ext_ref[layer, r, :, h * H : (h + 1) * H] = ext
                passing = jnp.exp(-ext * path)
                weight = through[h] * (1.0 - passing)
                colours = []
                for c in range(3):
                    lit = weight * jax.nn.sigmoid(polynomial(transfer_ref, c + 1, s))
                    colours.append(base[h][c] + lit)
                    gain_ref[layer, r, c, :, h * H : (h + 1) * H] = lit * shading
                b_out.append(tuple(colours))
                t_out.append(through[h] * passing)
            new.append((tuple(t_out), tuple(b_out)))
        return tuple(new)

    one, zero = jnp.ones((S, H), F32), jnp.zeros((S, H), F32)
    init = tuple(((one, one), ((zero,) * 3, (zero,) * 3)) for _ in range(layers))
    final = lax.fori_loop(0, rows, row, init)
    for layer in range(layers):
        through, base = final[layer]
        for h in range(2):
            for c in range(3):
                base_ref[layer, c, :, h * H : (h + 1) * H] = 0.2 * base[h][c]
            base_ref[layer, 3, :, h * H : (h + 1) * H] = 1.0 - through[h]


def shade_kernel(front_ref, ext_ref, gain_ref, base_ref, absorb_ref, send_ref, tmp):
    layers, rows = ext_ref.shape[0], ext_ref.shape[1]
    scale = [-absorb_ref[c] / 32.0 for c in range(3)]

    def pair(i, carry):
        acc = [list(x) for x in carry]
        for q in range(2):
            r = 2 * i + q
            for c in range(3):
                a, b = halves(front_ref[i, c, q].astype(F32))
                for layer in range(layers):
                    ga, gb = halves(gain_ref[layer, r, c])
                    acc[layer][2 * c] += a * ga
                    acc[layer][2 * c + 1] += b * gb
                    if layer < layers - 1:
                        ea, eb = halves(ext_ref[layer, r])
                        a, b = blur(a * jnp.exp(scale[c] * ea), b * jnp.exp(scale[c] * eb))
        return tuple(tuple(x) for x in acc)

    init = tuple(
        tuple(base_ref[layer, c, :, h * H : (h + 1) * H] for c in range(3) for h in range(2))
        for layer in range(layers)
    )
    final = lax.fori_loop(0, rows // 2, pair, init)
    for layer in range(layers):
        for h in range(2):
            for c in range(4):
                if c < 3:
                    tmp[layer, c, h] = final[layer][2 * c + h]
                else:
                    tmp[layer, c, h] = base_ref[layer, 3, :, h * H : (h + 1) * H]
                for j in range(4):
                    send_ref[2 * j + h, c, 2 * layer : 2 * layer + 2, :] = tmp[layer, c, h, pl.ds(j, 2, stride=4), :]


def merge_kernel(parts_ref, sign_ref, send_ref):
    count = parts_ref.shape[0]
    back = sign_ref[0] < 0.0
    through, colour = None, None
    for i in range(count):
        k = jnp.where(back, count - 1 - i, i)
        part = [parts_ref[k, c] for c in range(4)]
        if colour is None:
            colour, through = part[:3], 1.0 - part[3]
        else:
            colour = [colour[c] + through * part[c] for c in range(3)]
            through = through * (1.0 - part[3])
    for c in range(3):
        send_ref[:, c, :] = colour[c]
    send_ref[:, 3, :] = 1.0 - through


def final_kernel(parts_ref, sign_ref, out_ref):
    count = parts_ref.shape[0]
    back = sign_ref[0] < 0.0
    held = None
    for i in range(count):
        k = jnp.where(back, count - 1 - i, i)
        part = parts_ref[k]
        held = part if held is None else held + (1.0 - held[3:4]) * part
    out_ref[...] = held


def body(density, occupied, view_sign, transfer, absorb, light_in):
    layers, rows, columns = density.shape
    lights = lax.axis_size("light")
    views = lax.axis_size("view")
    pos = lax.axis_index("light").astype(jnp.int32)[None]
    sds = jax.ShapeDtypeStruct

    cells, first, last, send, light_rows = pl.pallas_call(
        prepare_kernel,
        out_shape=(
            sds((layers, rows, S, T), BF16),
            sds((rows, S, T), BF16),
            sds((rows, S, T), BF16),
            sds((lights, layers, 2, S, T), BF16),
            sds((3, 2, S, T), F32),
        ),
        in_specs=[VMEM, SMEM, VMEM, SMEM],
        out_specs=(VMEM,) * 5,
        scratch_shapes=[pltpu.VMEM((2 * rows * S, H), F32)],
        name="prepare",
    )(density, occupied, light_in, pos)

    ends = lights - 1
    low = lax.ppermute(last, "light", [(i, i + 1) for i in range(ends)])
    high = lax.ppermute(first, "light", [(i + 1, i) for i in range(ends)])
    recv = lax.all_to_all(send, "light", 0, 0)

    ext, gain, base = pl.pallas_call(
        lambda *refs: local_kernel(*refs, total_y=rows * views),
        out_shape=(
            sds((layers, rows, S, T), F32),
            sds((layers, rows, 3, S, T), F32),
            sds((layers, 4, S, T), F32),
        ),
        in_specs=[VMEM, VMEM, VMEM, SMEM, SMEM, SMEM],
        out_specs=(VMEM,) * 3,
        name="local",
    )(cells, low, high, occupied, view_sign, transfer)

    fronts = pl.pallas_call(
        propagate_kernel,
        out_shape=sds((lights, 3, 2, S, T), BF16),
        in_specs=[VMEM, VMEM, SMEM, SMEM],
        out_specs=VMEM,
        name="propagate",
    )(recv, light_rows, transfer, absorb)
    front = lax.all_to_all(fronts, "light", 0, 0)

    partial = pl.pallas_call(
        shade_kernel,
        out_shape=sds((8, 4, 8, H), F32),
        in_specs=[VMEM, VMEM, VMEM, VMEM, SMEM],
        out_specs=VMEM,
        scratch_shapes=[pltpu.VMEM((layers, 4, 2, S, H), F32)],
        name="shade",
    )(front, ext, gain, base, absorb)

    near = [[z * 8 + k for k in range(8)] for z in range(views // 8)]
    far = [[z * 8 + k for z in range(views // 8)] for k in range(8)]
    parts = lax.all_to_all(partial, "view", 0, 0, axis_index_groups=near)
    merged = pl.pallas_call(
        merge_kernel,
        out_shape=sds((8, 4, H), F32),
        in_specs=[VMEM, SMEM],
        out_specs=VMEM,
        name="merge",
    )(parts, view_sign)
    parts = lax.all_to_all(merged, "view", 0, 0, axis_index_groups=far)
    return pl.pallas_call(
        final_kernel,
        out_shape=sds((4, H), F32),
        in_specs=[VMEM, SMEM],
        out_specs=VMEM,
        name="final",
    )(parts, view_sign)


def solution(mesh):
    in_specs = (
        P("light", "view", None),
        P("light", "view", None),
        P(),
        P(),
        P(),
        P(None, "view", None),
    )
    out_specs = P(None, ("light", "view"))
    return jax.shard_map(body, mesh=mesh, in_specs=in_specs, out_specs=out_specs, check_vma=False)
```

```python
import jax
import jax.numpy as jnp
from jax import lax
from jax.experimental import pallas as pl
from jax.experimental.pallas import tpu as pltpu
from jax.sharding import PartitionSpec as P


S = 8
T = 256
H = 128
F32 = jnp.float32
BF16 = jnp.bfloat16
VMEM = pl.BlockSpec(memory_space=pltpu.VMEM)
LIMIT = pltpu.CompilerParams(vmem_limit_bytes=16 << 20)
SMEM = pl.BlockSpec(memory_space=pltpu.SMEM)


def halves(x):
    return x[..., :H], x[..., H:]


def lane_is(pos):
    return lax.broadcasted_iota(jnp.int32, (S, H), 1) == pos


def sub_is(pos):
    return lax.broadcasted_iota(jnp.int32, (S, H), 0) == pos


def previous(a, b):
    ra, rb = pltpu.roll(a, 1, a.ndim - 1), pltpu.roll(b, 1, a.ndim - 1)
    wrap = jnp.where(sub_is(0), 0.0, pltpu.roll(rb, 1, a.ndim - 2))
    first = lane_is(0)
    return jnp.where(first, wrap, ra), jnp.where(first, ra, rb)


def following(a, b):
    ra, rb = pltpu.roll(a, H - 1, a.ndim - 1), pltpu.roll(b, H - 1, a.ndim - 1)
    wrap = jnp.where(sub_is(S - 1), 0.0, pltpu.roll(ra, S - 1, a.ndim - 2))
    last = lane_is(H - 1)
    return jnp.where(last, rb, ra), jnp.where(last, wrap, rb)


def blur(a, b):
    pa, pb = previous(a, b)
    na, nb = following(a, b)
    return 0.25 * (pa + na) + 0.5 * a, 0.25 * (pb + nb) + 0.5 * b


def polynomial(coeffs, row, s):
    return coeffs[row, 0] + s * (coeffs[row, 1] + s * (coeffs[row, 2] + s * coeffs[row, 3]))


def softplus(x):
    u = jnp.exp(-jnp.abs(x))
    tail = jnp.where(u < 2.0**-8, u * (1.0 - u * (0.5 - u * (1.0 / 3.0))), jnp.log(1.0 + u))
    return jnp.maximum(x, 0.0) + tail


def brick_mask(occ_ref):
    sub = lax.broadcasted_iota(jnp.int32, (S, H), 0)
    out = []
    for h in range(2):
        occ = jnp.zeros((S, H), F32)
        for s in range(S):
            occ = jnp.where(sub == s, occ_ref[0, 0, 2 * s + h].astype(F32), occ)
        out.append(occ)
    return out


def prepare_kernel(dens_ref, occ_ref, cells_ref, first_ref, last_ref, send_ref, tmp):
    layers, rows, _ = dens_ref.shape
    occ = brick_mask(occ_ref)
    mask = jnp.concatenate(occ, axis=1)[None] > 0.5
    for layer in range(layers):
        x = dens_ref[layer].astype(F32)
        for s in range(S):
            for h in range(2):
                column = (2 * s + h) * H
                tmp[pl.ds(h * rows * S + s, rows, stride=S), :] = x[:, column : column + H]
        y = jnp.concatenate([tmp[h * rows * S : (h + 1) * rows * S, :].reshape(rows, S, H) for h in range(2)], axis=2)
        raw = y.astype(BF16)
        cells_ref[layer] = raw
        if layer == 0:
            first_ref[...] = raw
        if layer == layers - 1:
            last_ref[...] = raw
        masked = jnp.where(mask, y, -1.0).astype(BF16)
        send_ref[:, layer] = masked.reshape(rows // 2, 2, S, T)


def propagate_kernel(recv_ref, rows_ref, transfer_ref, absorb_ref, send_ref):
    blocks, layers = recv_ref.shape[0], recv_ref.shape[1]
    scale = [-absorb_ref[c] / 32.0 for c in range(3)]

    def block(k, carry):
        front = list(carry)
        for c in range(3):
            a, b = front[c]
            send_ref[k, c, :, :, :H] = a.astype(BF16)
            send_ref[k, c, :, :, H:] = b.astype(BF16)
        for layer in range(layers):
            ext = []
            for d in halves(recv_ref[k, layer].astype(F32)):
                ext.append(jnp.where(d < 0.0, 0.0, softplus(polynomial(transfer_ref, 0, d))))
            for c in range(3):
                a, b = front[c]
                front[c] = blur(a * jnp.exp(scale[c] * ext[0]), b * jnp.exp(scale[c] * ext[1]))
        return tuple(front)

    init = tuple(halves(rows_ref[c]) for c in range(3))
    final = lax.fori_loop(0, blocks - 1, block, init)
    for c in range(3):
        send_ref[blocks - 1, c, :, :, :H] = final[c][0].astype(BF16)
        send_ref[blocks - 1, c, :, :, H:] = final[c][1].astype(BF16)


def local_kernel(
    cells_ref, low_ref, high_ref, light_ref, occ_ref, sign_ref, transfer_ref, pos_ref,
    ext_ref, gain_ref, base_ref, rows_ref, *, total_y,
):
    start = 2 * pos_ref[0]
    for c in range(3):
        for r in range(2):
            for s in range(S):
                rows_ref[c, r, s : s + 1, :] = light_ref[c, pl.ds(start + r, 1), s * T : (s + 1) * T]
    layers, rows = cells_ref.shape[0], cells_ref.shape[1]
    occ = brick_mask(occ_ref)
    sign = sign_ref[0]
    back = sign < 0.0
    path = (2.0 / total_y) / jnp.abs(jnp.full((S, H), sign, F32))

    def load(layer, r):
        if layer < 0:
            v = low_ref[r]
        elif layer >= layers:
            v = high_ref[r]
        else:
            v = cells_ref[layer, r]
        return halves(v.astype(F32))

    def row(i, carry):
        r = jnp.where(back, rows - 1 - i, i)
        up = jnp.minimum(r + 1, rows - 1)
        down = jnp.maximum(r - 1, 0)
        column = [load(layer, r) for layer in range(-1, layers + 1)]
        new = []
        for layer in range(layers):
            through, base = carry[layer]
            d = column[layer + 1]
            dn, dp = load(layer, up), load(layer, down)
            zp, zn = previous(*d), following(*d)
            t_out, b_out = [], []
            for h in range(2):
                s = d[h]
                gx = 0.5 * (column[layer + 2][h] - column[layer][h])
                gy = 0.5 * (dn[h] - dp[h])
                gz = 0.5 * (zn[h] - zp[h])
                facing = (0.8 * gx + 0.36 * gy + 0.48 * gz) * lax.rsqrt(1.0 + gx * gx + gy * gy + gz * gz)
                shading = 0.65 + 0.35 * facing
                ext = softplus(polynomial(transfer_ref, 0, s)) * occ[h]
                ext_ref[layer, r, :, h * H : (h + 1) * H] = ext
                passing = jnp.exp(-ext * path)
                weight = through[h] * (1.0 - passing)
                colours = []
                for c in range(3):
                    lit = weight * jax.nn.sigmoid(polynomial(transfer_ref, c + 1, s))
                    colours.append(base[h][c] + lit)
                    gain_ref[layer, r, c, :, h * H : (h + 1) * H] = lit * shading
                b_out.append(tuple(colours))
                t_out.append(through[h] * passing)
            new.append((tuple(t_out), tuple(b_out)))
        return tuple(new)

    one, zero = jnp.ones((S, H), F32), jnp.zeros((S, H), F32)
    init = tuple(((one, one), ((zero,) * 3, (zero,) * 3)) for _ in range(layers))
    final = lax.fori_loop(0, rows, row, init)
    for layer in range(layers):
        through, base = final[layer]
        for h in range(2):
            for c in range(3):
                base_ref[layer, c, :, h * H : (h + 1) * H] = 0.2 * base[h][c]
            base_ref[layer, 3, :, h * H : (h + 1) * H] = 1.0 - through[h]


def shade_kernel(front_ref, ext_ref, gain_ref, base_ref, absorb_ref, send_ref):
    layers, rows = ext_ref.shape[0], ext_ref.shape[1]
    scale = [-absorb_ref[c] / 32.0 for c in range(3)]

    def pair(i, carry):
        acc = [list(x) for x in carry]
        for q in range(2):
            r = 2 * i + q
            for c in range(3):
                a, b = halves(front_ref[i, c, q].astype(F32))
                for layer in range(layers):
                    ga, gb = halves(gain_ref[layer, r, c])
                    acc[layer][2 * c] += a * ga
                    acc[layer][2 * c + 1] += b * gb
                    if layer < layers - 1:
                        ea, eb = halves(ext_ref[layer, r])
                        a, b = blur(a * jnp.exp(scale[c] * ea), b * jnp.exp(scale[c] * eb))
        return tuple(tuple(x) for x in acc)

    init = tuple(
        tuple(base_ref[layer, c, :, h * H : (h + 1) * H] for c in range(3) for h in range(2))
        for layer in range(layers)
    )
    final = lax.fori_loop(0, rows // 2, pair, init)
    for layer in range(layers):
        for h in range(2):
            for c in range(4):
                value = final[layer][2 * c + h] if c < 3 else base_ref[layer, 3, :, h * H : (h + 1) * H]
                send_ref[pl.ds(layer * 64 + h * 4 + c, S, stride=8), :] = value


def merge_kernel(parts_ref, sign_ref, out_ref):
    back = sign_ref[0] < 0.0

    def over(near, far):
        through = 1.0 - near[3]
        return [near[c] + through * far[c] for c in range(4)]

    held = None
    for i in range(8):
        j = jnp.where(back, 7 - i, i)
        part = [parts_ref[pl.ds(4 * j + c, 8, stride=32), :] for c in range(4)]
        held = part if held is None else over(held, part)
    for step in (1, 2, 4):
        other = [pltpu.roll(x, 8 - step, 0) for x in held]
        near = [jnp.where(back, o, h) for o, h in zip(other, held)]
        far = [jnp.where(back, h, o) for o, h in zip(other, held)]
        held = over(near, far)
    for c in range(4):
        out_ref[c : c + 1, :] = held[c][:1]


def in_vmem(x):
    return pltpu.with_memory_space_constraint(x, pltpu.VMEM)


def body(density, occupied, view_sign, transfer, absorb, light_in):
    layers, rows, _ = density.shape
    lights = lax.axis_size("light")
    views = lax.axis_size("view")
    pos = lax.axis_index("light").astype(jnp.int32)[None]
    out = pltpu.VMEM

    cells, first, last, send = pl.pallas_call(
        prepare_kernel,
        out_shape=(
            out((layers, rows, S, T), BF16),
            out((rows, S, T), BF16),
            out((rows, S, T), BF16),
            out((lights, layers, 2, S, T), BF16),
        ),
        in_specs=[VMEM, SMEM],
        out_specs=(VMEM,) * 4,
        scratch_shapes=[pltpu.VMEM((2 * rows * S, H), F32)],
        compiler_params=LIMIT,
        name="prepare",
    )(density, occupied)

    ends = lights - 1
    low = lax.ppermute(last, "light", [(i, i + 1) for i in range(ends)])
    high = lax.ppermute(first, "light", [(i + 1, i) for i in range(ends)])
    recv = lax.all_to_all(send, "light", 0, 0)

    ext, gain, base, light_rows = pl.pallas_call(
        lambda *refs: local_kernel(*refs, total_y=rows * views),
        out_shape=(
            out((layers, rows, S, T), F32),
            out((layers, rows, 3, S, T), F32),
            out((layers, 4, S, T), F32),
            out((3, 2, S, T), F32),
        ),
        in_specs=[VMEM, VMEM, VMEM, VMEM, SMEM, SMEM, SMEM, SMEM],
        out_specs=(VMEM,) * 4,
        compiler_params=LIMIT,
        name="local",
    )(in_vmem(cells), in_vmem(low), in_vmem(high), light_in, occupied, view_sign, transfer, pos)

    fronts = pl.pallas_call(
        propagate_kernel,
        out_shape=out((lights, 3, 2, S, T), BF16),
        in_specs=[VMEM, VMEM, SMEM, SMEM],
        out_specs=VMEM,
        compiler_params=LIMIT,
        name="propagate",
    )(in_vmem(recv), in_vmem(light_rows), transfer, absorb)
    front = lax.all_to_all(fronts, "light", 0, 0)

    partial = pl.pallas_call(
        shade_kernel,
        out_shape=out((views * 4, H), F32),
        in_specs=[VMEM, VMEM, VMEM, VMEM, SMEM],
        out_specs=VMEM,
        compiler_params=LIMIT,
        name="shade",
    )(in_vmem(front), in_vmem(ext), in_vmem(gain), in_vmem(base), absorb)

    parts = lax.all_to_all(partial.reshape(views, 4, H), "view", 0, 0).reshape(views * 4, H)
    return pl.pallas_call(
        merge_kernel,
        out_shape=jax.ShapeDtypeStruct((4, H), F32),
        in_specs=[VMEM, SMEM],
        out_specs=VMEM,
        compiler_params=LIMIT,
        name="merge",
    )(in_vmem(parts), view_sign)


def solution(mesh):
    in_specs = (
        P("light", "view", None),
        P("light", "view", None),
        P(),
        P(),
        P(),
        P(None, "view", None),
    )
    out_specs = P(None, ("light", "view"))
    return jax.shard_map(body, mesh=mesh, in_specs=in_specs, out_specs=out_specs, check_vma=False)
```

```python
import jax
import jax.numpy as jnp
from jax import lax
from jax.experimental import pallas as pl
from jax.experimental.pallas import tpu as pltpu
from jax.sharding import PartitionSpec as P

S = 8
T = 256
H = 128
F32 = jnp.float32
BF16 = jnp.bfloat16
VMEM = pl.BlockSpec(memory_space=pltpu.VMEM)
ANY = pl.BlockSpec(memory_space=pl.ANY)
LIMIT = pltpu.CompilerParams(vmem_limit_bytes=16 << 20)
SMEM = pl.BlockSpec(memory_space=pltpu.SMEM)


def halves(x):
    return x[..., :H], x[..., H:]


def shifted(a, b, by, fill=0.0):
    ra, rb = pltpu.roll(a, by % H, a.ndim - 1), pltpu.roll(b, by % H, a.ndim - 1)
    lane = lax.broadcasted_iota(jnp.int32, (S, H), 1)
    sub = lax.broadcasted_iota(jnp.int32, (S, H), 0)
    if by > 0:
        wrap = jnp.where(sub == 0, fill, pltpu.roll(rb, 1, a.ndim - 2))
        return jnp.where(lane < by, wrap, ra), jnp.where(lane < by, ra, rb)
    wrap = jnp.where(sub == S - 1, fill, pltpu.roll(ra, S - 1, a.ndim - 2))
    return jnp.where(lane >= H + by, rb, ra), jnp.where(lane >= H + by, wrap, rb)


def tap(before, cell, after):
    return [0.25 * (p + n) + 0.5 * c for p, c, n in zip(before, cell, after)]


def blur(a, b):
    return tap(shifted(a, b, 1), (a, b), shifted(a, b, -1))


ABSORB, PATH, OCCUPANCY, PLANES = 16, 19, 20, 22


def polynomial(const_ref, row, s):
    c = [const_ref[4 * row + n] for n in range(4)]
    return c[0] + s * (c[1] + s * (c[2] + s * c[3]))


def softplus(x):
    u = jnp.exp(-jnp.abs(x))
    tail = jnp.where(u < 2.0**-8, u * (1.0 - u * (0.5 - u * (1.0 / 3.0))), jnp.log(1.0 + u))
    return jnp.maximum(x, 0.0) + tail


def brick_mask(occ_ref):
    sub = lax.broadcasted_iota(jnp.int32, (S, H), 0)
    out = []
    for h in range(2):
        occ = jnp.zeros((S, H), F32)
        for s in range(S):
            occ = jnp.where(sub == s, occ_ref[0, 0, 2 * s + h].astype(F32), occ)
        out.append(occ)
    return out


TINY = 2.0**-100


def prepare_kernel(
    dens_ref, occ_hbm, transfer_hbm, absorb_hbm, sign_ref, cells_ref, const_ref, send_ref,
    raw, packed, tmp, occ_ref, transfer_ref, absorb_ref, in_sem, out_sem, small_sem, *, total_y,
):
    layers, rows, _ = dens_ref.shape
    small = [
        pltpu.make_async_copy(src, dst, small_sem.at[n])
        for n, (src, dst) in enumerate(
            ((occ_hbm, occ_ref), (transfer_hbm, transfer_ref), (absorb_hbm, absorb_ref))
        )
    ]
    loads = [pltpu.make_async_copy(dens_ref.at[n], raw.at[n], in_sem.at[n]) for n in range(layers)]
    stores = [pltpu.make_async_copy(packed.at[:, n], send_ref.at[:, n], out_sem.at[n]) for n in range(layers)]
    for copy in small[:1] + loads + small[1:]:
        copy.start()
    small[0].wait()
    occ = brick_mask(occ_ref)
    mask = jnp.concatenate(occ, axis=1)[None] > 0.5
    for layer in range(layers):
        loads[layer].wait()
        x = raw[layer].astype(F32)
        for s in range(S):
            for h in range(2):
                column = (2 * s + h) * H
                tmp[layer, h, pl.ds(s, rows, stride=S), :] = x[:, column : column + H]
        y = jnp.concatenate([tmp[layer, h].reshape(rows, S, H) for h in range(2)], axis=2)
        cells_ref[layer] = y.astype(BF16)
        sent = jnp.where(mask, y, -jnp.maximum(y, TINY)).astype(BF16)
        packed[:, layer] = sent.reshape(rows // 2, 2, S, T)
        stores[layer].start()
    for copy in small[1:]:
        copy.wait()
    for row in range(4):
        for n in range(4):
            const_ref[4 * row + n] = jnp.full((S, H), transfer_ref[row, n], F32)
    for c in range(3):
        const_ref[ABSORB + c] = jnp.full((S, H), absorb_ref[c] * (-1.0 / 32.0), F32)
    const_ref[PATH] = (2.0 / total_y) / jnp.abs(jnp.full((S, H), sign_ref[0], F32))
    for h in range(2):
        const_ref[OCCUPANCY + h] = occ[h]
    for store in stores:
        store.wait()


def propagate_kernel(recv_ref, rows_ref, const_ref, send_ref):
    blocks, layers = recv_ref.shape[0], recv_ref.shape[1]
    scale = [const_ref[ABSORB + c] for c in range(3)]

    def density(k, layer):
        d = recv_ref[k, layer].astype(F32)
        return jnp.where(d >= 0.0, d, jnp.where(d > -2.0 * TINY, 0.0, -d)).astype(BF16)

    for k in range(blocks):
        send_ref[k, 3] = density(k - 1, layers - 1) if k > 0 else jnp.zeros((2, S, T), BF16)
        send_ref[k, 4] = density(k + 1, 0) if k < blocks - 1 else jnp.zeros((2, S, T), BF16)

    def extinction(k):
        out = []
        for layer in range(layers):
            for d in halves(recv_ref[k, layer].astype(F32)):
                out.append(jnp.where(d < 0.0, 0.0, softplus(polynomial(const_ref, 0, d))))
        return tuple(out)

    def emit(k, front):
        for c in range(3):
            send_ref[k, c, :, :, :H] = front[2 * c].astype(BF16)
            send_ref[k, c, :, :, H:] = front[2 * c + 1].astype(BF16)

    def block(k, carry):
        front, ext = list(carry[0]), carry[1]
        emit(k, front)
        for first in range(0, layers, 2):
            here, then = ext[2 * first : 2 * first + 2], ext[2 * first + 2 : 2 * first + 4]
            sides = [shifted(*then, 1, fill=1e30), then, shifted(*then, -1, fill=1e30)]
            for c in range(3):
                g = [f * jnp.exp(scale[c] * e) for f, e in zip(front[2 * c : 2 * c + 2], here)]
                g = [shifted(*g, 2), shifted(*g, 1), g, shifted(*g, -1), shifted(*g, -2)]
                lit = []
                for n in range(3):
                    arrived = tap(g[n], g[n + 1], g[n + 2])
                    lit.append([f * jnp.exp(scale[c] * e) for f, e in zip(arrived, sides[n])])
                front[2 * c : 2 * c + 2] = tap(*lit)
        return tuple(front), extinction(k + 1)

    init = tuple(x for c in range(3) for x in halves(rows_ref[c]))
    front, _ = lax.fori_loop(0, blocks - 1, block, (init, extinction(0)))
    emit(blocks - 1, front)


def local_kernel(
    cells_ref, light_ref, const_ref, sign_ref,
    ext_ref, gain_ref, slope_ref, base_ref, rows_ref, light, sem,
):
    layers, rows = cells_ref.shape[0], cells_ref.shape[1]
    load = pltpu.make_async_copy(light_ref, light, sem)
    load.start()
    occ = [const_ref[OCCUPANCY + h] for h in range(2)]
    back = sign_ref[0] < 0.0
    path = const_ref[PATH]

    def row(i, carry):
        r = jnp.where(back, rows - 1 - i, i)
        up = jnp.minimum(r + 1, rows - 1)
        down = jnp.maximum(r - 1, 0)
        column = [halves(cells_ref[layer, r].astype(F32)) for layer in range(layers)]
        new = []
        for layer in range(layers):
            through, base = carry[layer]
            d = column[layer]
            dn = halves(cells_ref[layer, up].astype(F32))
            dp = halves(cells_ref[layer, down].astype(F32))
            zp, zn = shifted(*d, 1), shifted(*d, -1)
            t_out, b_out = [], []
            for h in range(2):
                at = slice(h * H, (h + 1) * H)
                s = d[h]
                gy = 0.5 * (dn[h] - dp[h])
                gz = 0.5 * (zn[h] - zp[h])
                side, length = 0.36 * gy + 0.48 * gz, 1.0 + gy * gy + gz * gz
                if 0 < layer < layers - 1:
                    gx = 0.5 * (column[layer + 1][h] - column[layer - 1][h])
                    shading = 0.65 + 0.35 * ((0.8 * gx + side) * lax.rsqrt(length + gx * gx))
                else:
                    edge = 0 if layer == 0 else 1
                    slope_ref[edge, 0, r, :, at] = side
                    slope_ref[edge, 1, r, :, at] = length
                    shading = None
                ext = softplus(polynomial(const_ref, 0, s)) * occ[h]
                ext_ref[layer, r, :, at] = ext
                passing = jnp.exp(-ext * path)
                weight = through[h] * (1.0 - passing)
                colours = []
                for c in range(3):
                    lit = weight * jax.nn.sigmoid(polynomial(const_ref, c + 1, s))
                    colours.append(base[h][c] + lit)
                    gain_ref[layer, r, c, :, at] = lit if shading is None else lit * shading
                b_out.append(tuple(colours))
                t_out.append(through[h] * passing)
            new.append((tuple(t_out), tuple(b_out)))
        return tuple(new)

    one, zero = jnp.ones((S, H), F32), jnp.zeros((S, H), F32)
    init = tuple(((one, one), ((zero,) * 3, (zero,) * 3)) for _ in range(layers))
    final = lax.fori_loop(0, rows, row, init)
    for layer in range(layers):
        through, base = final[layer]
        for h in range(2):
            for c in range(3):
                base_ref[layer, c, :, h * H : (h + 1) * H] = 0.2 * base[h][c]
            base_ref[layer, 3, :, h * H : (h + 1) * H] = 1.0 - through[h]
    load.wait()
    start = 2 * lax.axis_index("light")
    for c in range(3):
        for r in range(2):
            for s in range(S):
                rows_ref[c, r, s : s + 1, :] = light[c, pl.ds(start + r, 1), s * T : (s + 1) * T]


def shade_kernel(front_ref, cells_ref, ext_ref, gain_ref, slope_ref, base_ref, const_ref, send_ref, shade):
    layers, rows = ext_ref.shape[0], ext_ref.shape[1]

    def finish(i, carry):
        for q in range(2):
            r = 2 * i + q
            for edge in range(2):
                low = front_ref[i, 3, q] if edge == 0 else cells_ref[layers - 2, r]
                high = cells_ref[1, r] if edge == 0 else front_ref[i, 4, q]
                gx = 0.5 * (high.astype(F32) - low.astype(F32))
                facing = (0.8 * gx + slope_ref[edge, 0, r]) * lax.rsqrt(slope_ref[edge, 1, r] + gx * gx)
                shade[edge, r] = 0.65 + 0.35 * facing
        return carry

    lax.fori_loop(0, rows // 2, finish, 0)

    def channel(c, carry):
        scale = const_ref[ABSORB + c]
        front = [halves(front_ref[r // 2, c, r % 2].astype(F32)) for r in range(rows)]
        for layer in range(layers):
            total = list(halves(base_ref[layer, c]))
            for r in range(rows):
                gain = halves(gain_ref[layer, r, c])
                if layer in (0, layers - 1):
                    gain = [g * s for g, s in zip(gain, halves(shade[min(layer, 1), r]))]
                total = [x + f * g for x, f, g in zip(total, front[r], gain)]
                if layer < layers - 1:
                    ext = halves(ext_ref[layer, r])
                    front[r] = blur(*[f * jnp.exp(scale * e) for f, e in zip(front[r], ext)])
            for h in range(2):
                send_ref[pl.ds(layer * 64 + h * 4 + c, S, stride=8), :] = total[h]
        return carry

    lax.fori_loop(0, 3, channel, 0)
    for layer in range(layers):
        for h in range(2):
            send_ref[pl.ds(layer * 64 + h * 4 + 3, S, stride=8), :] = base_ref[layer, 3, :, h * H : (h + 1) * H]


def merge_kernel(parts_ref, sign_ref, out_ref):
    back = sign_ref[0] < 0.0

    def over(near, far):
        through = 1.0 - near[3]
        return [near[c] + through * far[c] for c in range(4)]

    held = None
    for i in range(8):
        j = jnp.where(back, 7 - i, i)
        part = [parts_ref[pl.ds(4 * j + c, 8, stride=32), :] for c in range(4)]
        held = part if held is None else over(held, part)
    for step in (1, 2, 4):
        other = [pltpu.roll(x, 8 - step, 0) for x in held]
        near = [jnp.where(back, o, h) for o, h in zip(other, held)]
        far = [jnp.where(back, h, o) for o, h in zip(other, held)]
        held = over(near, far)
    for c in range(4):
        out_ref[c : c + 1, :] = held[c][:1]


def in_vmem(x):
    return pltpu.with_memory_space_constraint(x, pltpu.VMEM)


def in_hbm(x):
    return pltpu.with_memory_space_constraint(x, pltpu.HBM)


def body(density, occupied, view_sign, transfer, absorb, light_in):
    layers, rows, columns = density.shape
    lights = lax.axis_size("light")
    views = lax.axis_size("view")
    out = pltpu.VMEM
    small = (occupied, transfer, absorb)

    cells, const, send = pl.pallas_call(
        lambda *refs: prepare_kernel(*refs, total_y=rows * views),
        out_shape=(
            out((layers, rows, S, T), BF16),
            out((PLANES, S, H), F32),
            pltpu.HBM((lights, layers, 2, S, T), BF16),
        ),
        in_specs=[ANY] * 4 + [SMEM],
        out_specs=(VMEM, VMEM, ANY),
        scratch_shapes=[
            pltpu.VMEM((layers, rows, columns), BF16),
            pltpu.VMEM((lights, layers, 2, S, T), BF16),
            pltpu.VMEM((layers, 2, rows * S, H), F32),
            *[pltpu.SMEM(x.shape, x.dtype) for x in small],
            pltpu.SemaphoreType.DMA((layers,)),
            pltpu.SemaphoreType.DMA((layers,)),
            pltpu.SemaphoreType.DMA((len(small),)),
        ],
        compiler_params=LIMIT,
        name="prepare",
    )(*[in_hbm(x) for x in (density, *small)], view_sign)
    const = in_vmem(const)

    recv = lax.all_to_all(send, "light", 0, 0)

    ext, gain, slope, base, light_rows = pl.pallas_call(
        local_kernel,
        out_shape=(
            out((layers, rows, S, T), F32),
            out((layers, rows, 3, S, T), F32),
            out((2, 2, rows, S, T), F32),
            out((layers, 4, S, T), F32),
            out((3, 2, S, T), F32),
        ),
        in_specs=[VMEM, ANY, VMEM, SMEM],
        out_specs=(VMEM,) * 5,
        scratch_shapes=[pltpu.VMEM(light_in.shape, F32), pltpu.SemaphoreType.DMA(())],
        compiler_params=LIMIT,
        name="local",
    )(in_vmem(cells), in_hbm(light_in), const, view_sign)

    fronts = pl.pallas_call(
        propagate_kernel,
        out_shape=out((lights, 5, 2, S, T), BF16),
        in_specs=[VMEM, VMEM, VMEM],
        out_specs=VMEM,
        compiler_params=LIMIT,
        name="propagate",
    )(in_vmem(recv), in_vmem(light_rows), const)
    front = lax.all_to_all(fronts, "light", 0, 0)

    partial = pl.pallas_call(
        shade_kernel,
        out_shape=out((views * 4, H), F32),
        in_specs=[VMEM] * 7,
        out_specs=VMEM,
        scratch_shapes=[pltpu.VMEM((2, rows, S, T), F32)],
        compiler_params=LIMIT,
        name="shade",
    )(*[in_vmem(x) for x in (front, cells, ext, gain, slope, base)], const)

    parts = lax.all_to_all(partial.reshape(views, 4, H), "view", 0, 0).reshape(views * 4, H)
    return pl.pallas_call(
        merge_kernel,
        out_shape=jax.ShapeDtypeStruct((4, H), F32),
        in_specs=[VMEM, SMEM],
        out_specs=VMEM,
        compiler_params=LIMIT,
        name="merge",
    )(in_vmem(parts), view_sign)


def solution(mesh):
    in_specs = (
        P("light", "view", None),
        P("light", "view", None),
        P(),
        P(),
        P(),
        P(None, "view", None),
    )
    out_specs = P(None, ("light", "view"))
    return jax.shard_map(body, mesh=mesh, in_specs=in_specs, out_specs=out_specs, check_vma=False)
```

```python
import jax
import jax.numpy as jnp
from jax import lax
from jax.experimental import pallas as pl
from jax.experimental.pallas import tpu as pltpu
from jax.sharding import PartitionSpec as P

S = 8
T = 256
H = 128
F32 = jnp.float32
BF16 = jnp.bfloat16
VMEM = pl.BlockSpec(memory_space=pltpu.VMEM)
ANY = pl.BlockSpec(memory_space=pl.ANY)
LIMIT = pltpu.CompilerParams(vmem_limit_bytes=16 << 20)
SMEM = pl.BlockSpec(memory_space=pltpu.SMEM)


LIGHT_FIRST, LIGHT_STEP = 5, 1
VIEW_TURN = 3


def light_slot(k):
    return (LIGHT_STEP * (k - LIGHT_FIRST)) & 7


def halves(x):
    return x[..., :H], x[..., H:]


def shifted(a, b, by, fill=0.0):
    ra, rb = pltpu.roll(a, by % H, a.ndim - 1), pltpu.roll(b, by % H, a.ndim - 1)
    lane = lax.broadcasted_iota(jnp.int32, (S, H), 1)
    sub = lax.broadcasted_iota(jnp.int32, (S, H), 0)
    if by > 0:
        wrap = jnp.where(sub == S - 1, fill, pltpu.roll(rb, S - 1, a.ndim - 2))
        return jnp.where(lane < by, wrap, ra), jnp.where(lane < by, ra, rb)
    wrap = jnp.where(sub == 0, fill, pltpu.roll(ra, 1, a.ndim - 2))
    return jnp.where(lane >= H + by, rb, ra), jnp.where(lane >= H + by, wrap, rb)


def tap(before, cell, after):
    return [0.25 * (p + n) + 0.5 * c for p, c, n in zip(before, cell, after)]


def blur(a, b):
    return tap(shifted(a, b, 1), (a, b), shifted(a, b, -1))


ABSORB, PATH, OCCUPANCY, PLANES = 16, 19, 20, 22


def polynomial(const_ref, row, s):
    c = [const_ref[4 * row + n] for n in range(4)]
    return c[0] + s * (c[1] + s * (c[2] + s * c[3]))


def softplus(x):
    u = jnp.exp(-jnp.abs(x))
    tail = jnp.where(u < 2.0**-8, u * (1.0 - u * (0.5 - u * (1.0 / 3.0))), jnp.log(1.0 + u))
    return jnp.maximum(x, 0.0) + tail


def brick_mask(occ_ref):
    sub = lax.broadcasted_iota(jnp.int32, (S, H), 0)
    out = []
    for h in range(2):
        occ = jnp.zeros((S, H), F32)
        for s in range(S):
            occ = jnp.where(sub == s, occ_ref[0, 0, 2 * (S - 1 - s) + h].astype(F32), occ)
        out.append(occ)
    return out


TINY = 2.0**-100


def prepare_kernel(
    dens_ref, occ_hbm, transfer_hbm, absorb_hbm, sign_ref, cells_ref, const_ref, send_ref,
    raw, packed, tmp, occ_ref, transfer_ref, absorb_ref, in_sem, out_sem, small_sem, *, total_y,
):
    layers, rows, _ = dens_ref.shape
    small = [
        pltpu.make_async_copy(src, dst, small_sem.at[n])
        for n, (src, dst) in enumerate(
            ((occ_hbm, occ_ref), (transfer_hbm, transfer_ref), (absorb_hbm, absorb_ref))
        )
    ]
    loads = [pltpu.make_async_copy(dens_ref.at[n], raw.at[n], in_sem.at[n]) for n in range(layers)]
    stores = [pltpu.make_async_copy(packed.at[:, n], send_ref.at[:, n], out_sem.at[n]) for n in range(layers)]
    for copy in small[:1] + loads + small[1:]:
        copy.start()
    small[0].wait()
    occ = brick_mask(occ_ref)
    mask = jnp.concatenate(occ, axis=1)[None] > 0.5
    for layer in range(layers):
        loads[layer].wait()
        x = raw[layer].astype(F32)
        for s in range(S):
            for h in range(2):
                column = (2 * (S - 1 - s) + h) * H
                tmp[layer, h, pl.ds(s, rows, stride=S), :] = x[:, column : column + H]
        y = jnp.concatenate([tmp[layer, h].reshape(rows, S, H) for h in range(2)], axis=2)
        cells_ref[layer] = y.astype(BF16)
        sent = jnp.where(mask, y, -jnp.maximum(y, TINY)).astype(BF16)
        for k in range(rows // 2):
            packed[light_slot(k), layer] = sent[2 * k : 2 * k + 2]
        stores[layer].start()
    for copy in small[1:]:
        copy.wait()
    for row in range(4):
        for n in range(4):
            const_ref[4 * row + n] = jnp.full((S, H), transfer_ref[row, n], F32)
    for c in range(3):
        const_ref[ABSORB + c] = jnp.full((S, H), absorb_ref[c] * (-1.0 / 32.0), F32)
    const_ref[PATH] = (2.0 / total_y) / jnp.abs(jnp.full((S, H), sign_ref[0], F32))
    for h in range(2):
        const_ref[OCCUPANCY + h] = occ[h]
    for store in stores:
        store.wait()


def propagate_kernel(recv_ref, rows_ref, const_ref, send_ref):
    blocks, layers = recv_ref.shape[0], recv_ref.shape[1]
    scale = [const_ref[ABSORB + c] for c in range(3)]

    def density(slot, layer):
        d = recv_ref[slot, layer].astype(F32)
        return jnp.where(d >= 0.0, d, jnp.where(d > -2.0 * TINY, 0.0, -d)).astype(BF16)

    for k in range(blocks):
        slot, none = light_slot(k), jnp.zeros((2, S, T), BF16)
        send_ref[slot, 3] = density(light_slot(k - 1), layers - 1) if k > 0 else none
        send_ref[slot, 4] = density(light_slot(k + 1), 0) if k < blocks - 1 else none

    def extinction(k):
        out = []
        for layer in range(layers):
            for d in halves(recv_ref[light_slot(k), layer].astype(F32)):
                out.append(jnp.where(d < 0.0, 0.0, softplus(polynomial(const_ref, 0, d))))
        return tuple(out)

    def emit(k, front):
        for c in range(3):
            send_ref[light_slot(k), c, :, :, :H] = front[2 * c].astype(BF16)
            send_ref[light_slot(k), c, :, :, H:] = front[2 * c + 1].astype(BF16)

    def block(k, carry):
        front, ext = list(carry[0]), carry[1]
        emit(k, front)
        for first in range(0, layers, 2):
            here, then = ext[2 * first : 2 * first + 2], ext[2 * first + 2 : 2 * first + 4]
            sides = [shifted(*then, 1, fill=1e30), then, shifted(*then, -1, fill=1e30)]
            for c in range(3):
                g = [f * jnp.exp(scale[c] * e) for f, e in zip(front[2 * c : 2 * c + 2], here)]
                g = [shifted(*g, 2), shifted(*g, 1), g, shifted(*g, -1), shifted(*g, -2)]
                lit = []
                for n in range(3):
                    arrived = tap(g[n], g[n + 1], g[n + 2])
                    lit.append([f * jnp.exp(scale[c] * e) for f, e in zip(arrived, sides[n])])
                front[2 * c : 2 * c + 2] = tap(*lit)
        return tuple(front), extinction(k + 1)

    init = tuple(x for c in range(3) for x in halves(rows_ref[c]))
    front, _ = lax.fori_loop(0, blocks - 1, block, (init, extinction(0)))
    emit(blocks - 1, front)


def local_kernel(
    cells_ref, light_ref, const_ref, sign_ref,
    ext_ref, gain_ref, slope_ref, base_ref, rows_ref, light, sem,
):
    layers, rows = cells_ref.shape[0], cells_ref.shape[1]
    load = pltpu.make_async_copy(light_ref, light, sem)
    load.start()
    occ = [const_ref[OCCUPANCY + h] for h in range(2)]
    back = sign_ref[0] < 0.0
    path = const_ref[PATH]

    def row(i, carry):
        r = jnp.where(back, rows - 1 - i, i)
        up = jnp.minimum(r + 1, rows - 1)
        down = jnp.maximum(r - 1, 0)
        column = [halves(cells_ref[layer, r].astype(F32)) for layer in range(layers)]
        new = []
        for layer in range(layers):
            through, base = carry[layer]
            d = column[layer]
            dn = halves(cells_ref[layer, up].astype(F32))
            dp = halves(cells_ref[layer, down].astype(F32))
            zp, zn = shifted(*d, 1), shifted(*d, -1)
            t_out, b_out = [], []
            for h in range(2):
                at = slice(h * H, (h + 1) * H)
                s = d[h]
                gy = 0.5 * (dn[h] - dp[h])
                gz = 0.5 * (zn[h] - zp[h])
                side, length = 0.36 * gy + 0.48 * gz, 1.0 + gy * gy + gz * gz
                if 0 < layer < layers - 1:
                    gx = 0.5 * (column[layer + 1][h] - column[layer - 1][h])
                    shading = 0.65 + 0.35 * ((0.8 * gx + side) * lax.rsqrt(length + gx * gx))
                else:
                    edge = 0 if layer == 0 else 1
                    slope_ref[edge, 0, r, :, at] = side
                    slope_ref[edge, 1, r, :, at] = length
                    shading = None
                ext = softplus(polynomial(const_ref, 0, s)) * occ[h]
                ext_ref[layer, r, :, at] = ext
                passing = jnp.exp(-ext * path)
                weight = through[h] * (1.0 - passing)
                colours = []
                for c in range(3):
                    lit = weight * jax.nn.sigmoid(polynomial(const_ref, c + 1, s))
                    colours.append(base[h][c] + lit)
                    gain_ref[layer, r, c, :, at] = lit if shading is None else lit * shading
                b_out.append(tuple(colours))
                t_out.append(through[h] * passing)
            new.append((tuple(t_out), tuple(b_out)))
        return tuple(new)

    one, zero = jnp.ones((S, H), F32), jnp.zeros((S, H), F32)
    init = tuple(((one, one), ((zero,) * 3, (zero,) * 3)) for _ in range(layers))
    final = lax.fori_loop(0, rows, row, init)
    for layer in range(layers):
        through, base = final[layer]
        for h in range(2):
            for c in range(3):
                base_ref[layer, c, :, h * H : (h + 1) * H] = 0.2 * base[h][c]
            base_ref[layer, 3, :, h * H : (h + 1) * H] = 1.0 - through[h]
    load.wait()
    start = 2 * lax.axis_index("light")
    for c in range(3):
        for r in range(2):
            for s in range(S):
                rows_ref[c, r, s : s + 1, :] = light[c, pl.ds(start + r, 1), (S - 1 - s) * T : (S - s) * T]


def view_row(layer, h):
    return 64 * ((VIEW_TURN - layer) & 3) + 4 * (1 - h)


def shade_kernel(front_ref, cells_ref, ext_ref, gain_ref, slope_ref, base_ref, const_ref, send_ref, shade):
    layers, rows = ext_ref.shape[0], ext_ref.shape[1]

    def finish(i, carry):
        for q in range(2):
            r = 2 * i + q
            for edge in range(2):
                low = front_ref[light_slot(i), 3, q] if edge == 0 else cells_ref[layers - 2, r]
                high = cells_ref[1, r] if edge == 0 else front_ref[light_slot(i), 4, q]
                gx = 0.5 * (high.astype(F32) - low.astype(F32))
                facing = (0.8 * gx + slope_ref[edge, 0, r]) * lax.rsqrt(slope_ref[edge, 1, r] + gx * gx)
                shade[edge, r] = 0.65 + 0.35 * facing
        return carry

    lax.fori_loop(0, rows // 2, finish, 0)

    def channel(c, carry):
        scale = const_ref[ABSORB + c]
        front = [halves(front_ref[light_slot(r // 2), c, r % 2].astype(F32)) for r in range(rows)]
        for layer in range(layers):
            total = list(halves(base_ref[layer, c]))
            for r in range(rows):
                gain = halves(gain_ref[layer, r, c])
                if layer in (0, layers - 1):
                    gain = [g * s for g, s in zip(gain, halves(shade[min(layer, 1), r]))]
                total = [x + f * g for x, f, g in zip(total, front[r], gain)]
                if layer < layers - 1:
                    ext = halves(ext_ref[layer, r])
                    front[r] = blur(*[f * jnp.exp(scale * e) for f, e in zip(front[r], ext)])
            for h in range(2):
                send_ref[pl.ds(view_row(layer, h) + c, S, stride=8), :] = total[h]
        return carry

    lax.fori_loop(0, 3, channel, 0)
    for layer in range(layers):
        for h in range(2):
            send_ref[pl.ds(view_row(layer, h) + 3, S, stride=8), :] = base_ref[layer, 3, :, h * H : (h + 1) * H]


def merge_kernel(parts_ref, sign_ref, out_ref):
    back = sign_ref[0] >= 0.0

    def over(near, far):
        through = 1.0 - near[3]
        return [near[c] + through * far[c] for c in range(4)]

    held = None
    for i in range(8):
        j = jnp.where(back, 7 - i, i)
        part = [parts_ref[pl.ds(4 * j + c, 8, stride=32), :] for c in range(4)]
        held = part if held is None else over(held, part)
    if VIEW_TURN != 3:
        held = [pltpu.roll(x, 6 - 2 * VIEW_TURN, 0) for x in held]
    for step in (1, 2, 4):
        other = [pltpu.roll(x, 8 - step, 0) for x in held]
        near = [jnp.where(back, o, h) for o, h in zip(other, held)]
        far = [jnp.where(back, h, o) for o, h in zip(other, held)]
        held = over(near, far)
    for c in range(4):
        out_ref[c : c + 1, :] = held[c][:1]


def in_vmem(x):
    return pltpu.with_memory_space_constraint(x, pltpu.VMEM)


def in_hbm(x):
    return pltpu.with_memory_space_constraint(x, pltpu.HBM)


def body(density, occupied, view_sign, transfer, absorb, light_in):
    layers, rows, columns = density.shape
    lights = lax.axis_size("light")
    views = lax.axis_size("view")
    out = pltpu.VMEM
    small = (occupied, transfer, absorb)

    cells, const, send = pl.pallas_call(
        lambda *refs: prepare_kernel(*refs, total_y=rows * views),
        out_shape=(
            out((layers, rows, S, T), BF16),
            out((PLANES, S, H), F32),
            pltpu.HBM((lights, layers, 2, S, T), BF16),
        ),
        in_specs=[ANY] * 4 + [SMEM],
        out_specs=(VMEM, VMEM, ANY),
        scratch_shapes=[
            pltpu.VMEM((layers, rows, columns), BF16),
            pltpu.VMEM((lights, layers, 2, S, T), BF16),
            pltpu.VMEM((layers, 2, rows * S, H), F32),
            *[pltpu.SMEM(x.shape, x.dtype) for x in small],
            pltpu.SemaphoreType.DMA((layers,)),
            pltpu.SemaphoreType.DMA((layers,)),
            pltpu.SemaphoreType.DMA((len(small),)),
        ],
        compiler_params=LIMIT,
        name="prepare",
    )(*[in_hbm(x) for x in (density, *small)], view_sign)
    const = in_vmem(const)

    light_list = [sorted(range(lights), key=light_slot)]
    view_list = [[(16 * VIEW_TURN + 15 - k) % views for k in range(views)]]
    recv = lax.all_to_all(send, "light", 0, 0, axis_index_groups=light_list)

    ext, gain, slope, base, light_rows = pl.pallas_call(
        local_kernel,
        out_shape=(
            out((layers, rows, S, T), F32),
            out((layers, rows, 3, S, T), F32),
            out((2, 2, rows, S, T), F32),
            out((layers, 4, S, T), F32),
            out((3, 2, S, T), F32),
        ),
        in_specs=[VMEM, ANY, VMEM, SMEM],
        out_specs=(VMEM,) * 5,
        scratch_shapes=[pltpu.VMEM(light_in.shape, F32), pltpu.SemaphoreType.DMA(())],
        compiler_params=LIMIT,
        name="local",
    )(in_vmem(cells), in_hbm(light_in), const, view_sign)

    fronts = pl.pallas_call(
        propagate_kernel,
        out_shape=out((lights, 5, 2, S, T), BF16),
        in_specs=[VMEM, VMEM, VMEM],
        out_specs=VMEM,
        compiler_params=LIMIT,
        name="propagate",
    )(in_vmem(recv), in_vmem(light_rows), const)
    front = lax.all_to_all(fronts, "light", 0, 0, axis_index_groups=light_list)

    partial = pl.pallas_call(
        shade_kernel,
        out_shape=out((views * 4, H), F32),
        in_specs=[VMEM] * 7,
        out_specs=VMEM,
        scratch_shapes=[pltpu.VMEM((2, rows, S, T), F32)],
        compiler_params=LIMIT,
        name="shade",
    )(*[in_vmem(x) for x in (front, cells, ext, gain, slope, base)], const)

    parts = lax.all_to_all(partial.reshape(views, 4, H), "view", 0, 0, axis_index_groups=view_list)
    parts = parts.reshape(views * 4, H)
    return pl.pallas_call(
        merge_kernel,
        out_shape=jax.ShapeDtypeStruct((4, H), F32),
        in_specs=[VMEM, SMEM],
        out_specs=VMEM,
        compiler_params=LIMIT,
        name="merge",
    )(in_vmem(parts), view_sign)


def solution(mesh):
    in_specs = (
        P("light", "view", None),
        P("light", "view", None),
        P(),
        P(),
        P(),
        P(None, "view", None),
    )
    out_specs = P(None, ("light", "view"))
    return jax.shard_map(body, mesh=mesh, in_specs=in_specs, out_specs=out_specs, check_vma=False)
```

```python
import jax
import jax.numpy as jnp
from jax import lax
from jax.experimental import pallas as pl
from jax.experimental.pallas import tpu as pltpu
from jax.sharding import PartitionSpec as P

S = 8
T = 256
H = 128
F32 = jnp.float32
BF16 = jnp.bfloat16
VMEM = pl.BlockSpec(memory_space=pltpu.VMEM)
ANY = pl.BlockSpec(memory_space=pl.ANY)
LIMIT = pltpu.CompilerParams(vmem_limit_bytes=16 << 20)
SMEM = pl.BlockSpec(memory_space=pltpu.SMEM)


LIGHT_FIRST, LIGHT_STEP = 5, 1
VIEW_TURN = 3


def light_slot(k):
    return (LIGHT_STEP * (k - LIGHT_FIRST)) & 7


def halves(x):
    return x[..., :H], x[..., H:]


def shifted(a, b, by, fill=0.0):
    ra, rb = pltpu.roll(a, by % H, a.ndim - 1), pltpu.roll(b, by % H, a.ndim - 1)
    lane = lax.broadcasted_iota(jnp.int32, (S, H), 1)
    sub = lax.broadcasted_iota(jnp.int32, (S, H), 0)
    if by > 0:
        wrap = jnp.where(sub == S - 1, fill, pltpu.roll(rb, S - 1, a.ndim - 2))
        return jnp.where(lane < by, wrap, ra), jnp.where(lane < by, ra, rb)
    wrap = jnp.where(sub == 0, fill, pltpu.roll(ra, 1, a.ndim - 2))
    return jnp.where(lane >= H + by, rb, ra), jnp.where(lane >= H + by, wrap, rb)


def tap(before, cell, after):
    return [0.25 * (p + n) + 0.5 * c for p, c, n in zip(before, cell, after)]


def blur(a, b):
    return tap(shifted(a, b, 1), (a, b), shifted(a, b, -1))


ABSORB, PATH, OCCUPANCY, PLANES = 16, 19, 20, 22


def polynomial(const_ref, row, s):
    c = [const_ref[4 * row + n] for n in range(4)]
    return c[0] + s * (c[1] + s * (c[2] + s * c[3]))


def softplus(x):
    u = jnp.exp(-jnp.abs(x))
    tail = jnp.where(u < 2.0**-8, u * (1.0 - u * (0.5 - u * (1.0 / 3.0))), jnp.log(1.0 + u))
    return jnp.maximum(x, 0.0) + tail


def brick_mask(occ_ref):
    sub = lax.broadcasted_iota(jnp.int32, (S, H), 0)
    out = []
    for h in range(2):
        occ = jnp.zeros((S, H), F32)
        for s in range(S):
            occ = jnp.where(sub == s, occ_ref[0, 0, 2 * (S - 1 - s) + h].astype(F32), occ)
        out.append(occ)
    return out


def prepare_kernel(
    dens_ref, occ_hbm, transfer_hbm, absorb_hbm, sign_ref, cells_ref, const_ref, send_ref,
    raw, packed, tmp, occ_ref, transfer_ref, absorb_ref, in_sem, out_sem, small_sem, *, total_y,
):
    layers, rows, _ = dens_ref.shape
    small = [
        pltpu.make_async_copy(src, dst, small_sem.at[n])
        for n, (src, dst) in enumerate(
            ((occ_hbm, occ_ref), (transfer_hbm, transfer_ref), (absorb_hbm, absorb_ref))
        )
    ]
    loads = [pltpu.make_async_copy(dens_ref.at[n], raw.at[n], in_sem.at[n]) for n in range(layers)]
    stores = [pltpu.make_async_copy(packed.at[:, n], send_ref.at[:, n], out_sem.at[n]) for n in range(layers)]
    for copy in small[:1] + loads + small[1:]:
        copy.start()
    small[0].wait()
    occ = brick_mask(occ_ref)
    mask = jnp.concatenate(occ, axis=1)[None] > 0.5
    for layer in range(layers):
        loads[layer].wait()
        x = raw[layer].astype(F32)
        for s in range(S):
            for h in range(2):
                column = (2 * (S - 1 - s) + h) * H
                tmp[layer, h, pl.ds(s, rows, stride=S), :] = x[:, column : column + H]
        y = jnp.concatenate([tmp[layer, h].reshape(rows, S, H) for h in range(2)], axis=2)
        cells_ref[layer] = y.astype(BF16)
        sent = jnp.where(mask, y, -1.0).astype(BF16)
        for k in range(rows // 2):
            packed[light_slot(k), layer] = sent[2 * k : 2 * k + 2]
        stores[layer].start()
    for copy in small[1:]:
        copy.wait()
    for row in range(4):
        for n in range(4):
            const_ref[4 * row + n] = jnp.full((S, H), transfer_ref[row, n], F32)
    for c in range(3):
        const_ref[ABSORB + c] = jnp.full((S, H), absorb_ref[c] * (-1.0 / 32.0), F32)
    const_ref[PATH] = (2.0 / total_y) / jnp.abs(jnp.full((S, H), sign_ref[0], F32))
    for h in range(2):
        const_ref[OCCUPANCY + h] = occ[h]
    for store in stores:
        store.wait()


def propagate_kernel(recv_ref, rows_ref, const_ref, low_ref, high_ref, send_ref):
    del low_ref, high_ref
    blocks, layers = recv_ref.shape[0], recv_ref.shape[1]
    scale = [const_ref[ABSORB + c] for c in range(3)]

    def extinction(k):
        out = []
        for layer in range(layers):
            for d in halves(recv_ref[light_slot(k), layer].astype(F32)):
                out.append(jnp.where(d < 0.0, 0.0, softplus(polynomial(const_ref, 0, d))))
        return tuple(out)

    def emit(k, front):
        for c in range(3):
            send_ref[light_slot(k), c, :, :, :H] = front[2 * c].astype(BF16)
            send_ref[light_slot(k), c, :, :, H:] = front[2 * c + 1].astype(BF16)

    def block(k, carry):
        front, ext = list(carry[0]), carry[1]
        emit(k, front)
        for first in range(0, layers, 2):
            here, then = ext[2 * first : 2 * first + 2], ext[2 * first + 2 : 2 * first + 4]
            sides = [shifted(*then, 1, fill=1e30), then, shifted(*then, -1, fill=1e30)]
            for c in range(3):
                g = [f * jnp.exp(scale[c] * e) for f, e in zip(front[2 * c : 2 * c + 2], here)]
                g = [shifted(*g, 2), shifted(*g, 1), g, shifted(*g, -1), shifted(*g, -2)]
                lit = []
                for n in range(3):
                    arrived = tap(g[n], g[n + 1], g[n + 2])
                    lit.append([f * jnp.exp(scale[c] * e) for f, e in zip(arrived, sides[n])])
                front[2 * c : 2 * c + 2] = tap(*lit)
        return tuple(front), extinction(k + 1)

    init = tuple(x for c in range(3) for x in halves(rows_ref[c]))
    front, _ = lax.fori_loop(0, blocks - 1, block, (init, extinction(0)))
    emit(blocks - 1, front)


def local_kernel(
    cells_ref, light_ref, const_ref, sign_ref,
    ext_ref, gain_ref, slope_ref, base_ref, rows_ref, light, sem,
):
    layers, rows = cells_ref.shape[0], cells_ref.shape[1]
    load = pltpu.make_async_copy(light_ref, light, sem)
    load.start()
    occ = [const_ref[OCCUPANCY + h] for h in range(2)]
    back = sign_ref[0] < 0.0
    path = const_ref[PATH]

    def row(i, carry):
        r = jnp.where(back, rows - 1 - i, i)
        up = jnp.minimum(r + 1, rows - 1)
        down = jnp.maximum(r - 1, 0)
        column = [halves(cells_ref[layer, r].astype(F32)) for layer in range(layers)]
        new = []
        for layer in range(layers):
            through, base = carry[layer]
            d = column[layer]
            dn = halves(cells_ref[layer, up].astype(F32))
            dp = halves(cells_ref[layer, down].astype(F32))
            zp, zn = shifted(*d, 1), shifted(*d, -1)
            t_out, b_out = [], []
            for h in range(2):
                at = slice(h * H, (h + 1) * H)
                s = d[h]
                gy = 0.5 * (dn[h] - dp[h])
                gz = 0.5 * (zn[h] - zp[h])
                side, length = 0.36 * gy + 0.48 * gz, 1.0 + gy * gy + gz * gz
                if 0 < layer < layers - 1:
                    gx = 0.5 * (column[layer + 1][h] - column[layer - 1][h])
                    shading = 0.65 + 0.35 * ((0.8 * gx + side) * lax.rsqrt(length + gx * gx))
                else:
                    edge = 0 if layer == 0 else 1
                    slope_ref[edge, 0, r, :, at] = side
                    slope_ref[edge, 1, r, :, at] = length
                    shading = None
                ext = softplus(polynomial(const_ref, 0, s)) * occ[h]
                ext_ref[layer, r, :, at] = ext
                passing = jnp.exp(-ext * path)
                weight = through[h] * (1.0 - passing)
                colours = []
                for c in range(3):
                    lit = weight * jax.nn.sigmoid(polynomial(const_ref, c + 1, s))
                    colours.append(base[h][c] + lit)
                    gain_ref[layer, r, c, :, at] = lit if shading is None else lit * shading
                b_out.append(tuple(colours))
                t_out.append(through[h] * passing)
            new.append((tuple(t_out), tuple(b_out)))
        return tuple(new)

    one, zero = jnp.ones((S, H), F32), jnp.zeros((S, H), F32)
    init = tuple(((one, one), ((zero,) * 3, (zero,) * 3)) for _ in range(layers))
    final = lax.fori_loop(0, rows, row, init)
    for layer in range(layers):
        through, base = final[layer]
        for h in range(2):
            for c in range(3):
                base_ref[layer, c, :, h * H : (h + 1) * H] = 0.2 * base[h][c]
            base_ref[layer, 3, :, h * H : (h + 1) * H] = 1.0 - through[h]
    load.wait()
    start = 2 * lax.axis_index("light")
    for c in range(3):
        for r in range(2):
            for s in range(S):
                rows_ref[c, r, s : s + 1, :] = light[c, pl.ds(start + r, 1), (S - 1 - s) * T : (S - s) * T]


def view_row(layer, h):
    return 64 * ((VIEW_TURN - layer) & 3) + 4 * (1 - h)


def shade_kernel(front_ref, low_ref, high_ref, cells_ref, ext_ref, gain_ref, slope_ref, base_ref, const_ref, send_ref, shade):
    layers, rows = ext_ref.shape[0], ext_ref.shape[1]

    def finish(i, carry):
        for r in (2 * i, 2 * i + 1):
            for edge in range(2):
                low = low_ref[r] if edge == 0 else cells_ref[layers - 2, r]
                high = cells_ref[1, r] if edge == 0 else high_ref[r]
                gx = 0.5 * (high.astype(F32) - low.astype(F32))
                facing = (0.8 * gx + slope_ref[edge, 0, r]) * lax.rsqrt(slope_ref[edge, 1, r] + gx * gx)
                shade[edge, r] = 0.65 + 0.35 * facing
        return carry

    lax.fori_loop(0, rows // 2, finish, 0)

    def channel(c, carry):
        scale = const_ref[ABSORB + c]
        front = [halves(front_ref[light_slot(r // 2), c, r % 2].astype(F32)) for r in range(rows)]
        for layer in range(layers):
            total = list(halves(base_ref[layer, c]))
            for r in range(rows):
                gain = halves(gain_ref[layer, r, c])
                if layer in (0, layers - 1):
                    gain = [g * s for g, s in zip(gain, halves(shade[min(layer, 1), r]))]
                total = [x + f * g for x, f, g in zip(total, front[r], gain)]
                if layer < layers - 1:
                    ext = halves(ext_ref[layer, r])
                    front[r] = blur(*[f * jnp.exp(scale * e) for f, e in zip(front[r], ext)])
            for h in range(2):
                send_ref[pl.ds(view_row(layer, h) + c, S, stride=8), :] = total[h]
        return carry

    lax.fori_loop(0, 3, channel, 0)
    for layer in range(layers):
        for h in range(2):
            send_ref[pl.ds(view_row(layer, h) + 3, S, stride=8), :] = base_ref[layer, 3, :, h * H : (h + 1) * H]


def merge_kernel(parts_ref, sign_ref, out_ref):
    back = sign_ref[0] >= 0.0

    def over(near, far):
        through = 1.0 - near[3]
        return [near[c] + through * far[c] for c in range(4)]

    held = None
    for i in range(8):
        j = jnp.where(back, 7 - i, i)
        part = [parts_ref[pl.ds(4 * j + c, 8, stride=32), :] for c in range(4)]
        held = part if held is None else over(held, part)
    if VIEW_TURN != 3:
        held = [pltpu.roll(x, 6 - 2 * VIEW_TURN, 0) for x in held]
    for step in (1, 2, 4):
        other = [pltpu.roll(x, 8 - step, 0) for x in held]
        near = [jnp.where(back, o, h) for o, h in zip(other, held)]
        far = [jnp.where(back, h, o) for o, h in zip(other, held)]
        held = over(near, far)
    for c in range(4):
        out_ref[c : c + 1, :] = held[c][:1]


def in_vmem(x):
    return pltpu.with_memory_space_constraint(x, pltpu.VMEM)


def in_hbm(x):
    return pltpu.with_memory_space_constraint(x, pltpu.HBM)


def body(density, occupied, view_sign, transfer, absorb, light_in):
    layers, rows, columns = density.shape
    lights = lax.axis_size("light")
    views = lax.axis_size("view")
    out = pltpu.VMEM
    small = (occupied, transfer, absorb)

    cells, const, send = pl.pallas_call(
        lambda *refs: prepare_kernel(*refs, total_y=rows * views),
        out_shape=(
            out((layers, rows, S, T), BF16),
            out((PLANES, S, H), F32),
            pltpu.HBM((lights, layers, 2, S, T), BF16),
        ),
        in_specs=[ANY] * 4 + [SMEM],
        out_specs=(VMEM, VMEM, ANY),
        scratch_shapes=[
            pltpu.VMEM((layers, rows, columns), BF16),
            pltpu.VMEM((lights, layers, 2, S, T), BF16),
            pltpu.VMEM((layers, 2, rows * S, H), F32),
            *[pltpu.SMEM(x.shape, x.dtype) for x in small],
            pltpu.SemaphoreType.DMA((layers,)),
            pltpu.SemaphoreType.DMA((layers,)),
            pltpu.SemaphoreType.DMA((len(small),)),
        ],
        compiler_params=LIMIT,
        name="prepare",
    )(*[in_hbm(x) for x in (density, *small)], view_sign)
    const = in_vmem(const)

    light_list = [sorted(range(lights), key=light_slot)]
    view_list = [[(16 * VIEW_TURN + 15 - k) % views for k in range(views)]]
    ends = lights - 1
    first, last = cells[0], cells[layers - 1]
    low = lax.ppermute(last, "light", [(i, i + 1) for i in range(ends)])
    high = lax.ppermute(first, "light", [(i + 1, i) for i in range(ends)])
    recv = lax.all_to_all(send, "light", 0, 0, axis_index_groups=light_list)

    ext, gain, slope, base, light_rows = pl.pallas_call(
        local_kernel,
        out_shape=(
            out((layers, rows, S, T), F32),
            out((layers, rows, 3, S, T), F32),
            out((2, 2, rows, S, T), F32),
            out((layers, 4, S, T), F32),
            out((3, 2, S, T), F32),
        ),
        in_specs=[VMEM, ANY, VMEM, SMEM],
        out_specs=(VMEM,) * 5,
        scratch_shapes=[pltpu.VMEM(light_in.shape, F32), pltpu.SemaphoreType.DMA(())],
        compiler_params=LIMIT,
        name="local",
    )(in_vmem(cells), in_hbm(light_in), const, view_sign)

    fronts = pl.pallas_call(
        propagate_kernel,
        out_shape=out((lights, 3, 2, S, T), BF16),
        in_specs=[VMEM] * 5,
        out_specs=VMEM,
        compiler_params=LIMIT,
        name="propagate",
    )(in_vmem(recv), in_vmem(light_rows), const, in_vmem(low), in_vmem(high))
    front = lax.all_to_all(fronts, "light", 0, 0, axis_index_groups=light_list)

    partial = pl.pallas_call(
        shade_kernel,
        out_shape=out((views * 4, H), F32),
        in_specs=[VMEM] * 9,
        out_specs=VMEM,
        scratch_shapes=[pltpu.VMEM((2, rows, S, T), F32)],
        compiler_params=LIMIT,
        name="shade",
    )(*[in_vmem(x) for x in (front, low, high, cells, ext, gain, slope, base)], const)

    parts = lax.all_to_all(partial.reshape(views, 4, H), "view", 0, 0, axis_index_groups=view_list)
    parts = parts.reshape(views * 4, H)
    return pl.pallas_call(
        merge_kernel,
        out_shape=jax.ShapeDtypeStruct((4, H), F32),
        in_specs=[VMEM, SMEM],
        out_specs=VMEM,
        compiler_params=LIMIT,
        name="merge",
    )(in_vmem(parts), view_sign)


def solution(mesh):
    in_specs = (
        P("light", "view", None),
        P("light", "view", None),
        P(),
        P(),
        P(),
        P(None, "view", None),
    )
    out_specs = P(None, ("light", "view"))
    return jax.shard_map(body, mesh=mesh, in_specs=in_specs, out_specs=out_specs, check_vma=False)
```

```python
import jax
import jax.numpy as jnp
from jax import lax
from jax.experimental import pallas as pl
from jax.experimental.pallas import tpu as pltpu
from jax.sharding import PartitionSpec as P

S = 8
T = 256
H = 128
F32 = jnp.float32
BF16 = jnp.bfloat16
VMEM = pl.BlockSpec(memory_space=pltpu.VMEM)
ANY = pl.BlockSpec(memory_space=pl.ANY)
LIMIT = pltpu.CompilerParams(vmem_limit_bytes=16 << 20)
SMEM = pl.BlockSpec(memory_space=pltpu.SMEM)


CELLS_FIRST = 6
FRONT_FIRST = 4
VIEW_FIRST = 61


def light_slot(k, first):
    return (k - first) & 7


def halves(x):
    return x[..., :H], x[..., H:]


def shifted(a, b, by, fill=0.0):
    ra, rb = pltpu.roll(a, by % H, a.ndim - 1), pltpu.roll(b, by % H, a.ndim - 1)
    lane = lax.broadcasted_iota(jnp.int32, (S, H), 1)
    sub = lax.broadcasted_iota(jnp.int32, (S, H), 0)
    if by > 0:
        wrap = jnp.where(sub == S - 1, fill, pltpu.roll(rb, S - 1, a.ndim - 2))
        return jnp.where(lane < by, wrap, ra), jnp.where(lane < by, ra, rb)
    wrap = jnp.where(sub == 0, fill, pltpu.roll(ra, 1, a.ndim - 2))
    return jnp.where(lane >= H + by, rb, ra), jnp.where(lane >= H + by, wrap, rb)


def tap(before, cell, after):
    return [0.25 * (p + n) + 0.5 * c for p, c, n in zip(before, cell, after)]


def blur(a, b):
    return tap(shifted(a, b, 1), (a, b), shifted(a, b, -1))


ABSORB, PATH, OCCUPANCY, PLANES = 16, 19, 20, 22


def polynomial(const_ref, row, s):
    c = [const_ref[4 * row + n] for n in range(4)]
    return c[0] + s * (c[1] + s * (c[2] + s * c[3]))


def softplus(x):
    u = jnp.exp(-jnp.abs(x))
    tail = jnp.where(u < 2.0**-8, u * (1.0 - u * (0.5 - u * (1.0 / 3.0))), jnp.log(1.0 + u))
    return jnp.maximum(x, 0.0) + tail


def brick_mask(occ_ref):
    sub = lax.broadcasted_iota(jnp.int32, (S, H), 0)
    out = []
    for h in range(2):
        occ = jnp.zeros((S, H), F32)
        for s in range(S):
            occ = jnp.where(sub == s, occ_ref[0, 0, 2 * (S - 1 - s) + h].astype(F32), occ)
        out.append(occ)
    return out


def prepare_kernel(
    dens_ref, occ_hbm, transfer_hbm, absorb_hbm, sign_ref, cells_ref, const_ref, send_ref,
    raw, packed, tmp, occ_ref, transfer_ref, absorb_ref, in_sem, out_sem, small_sem, *, total_y,
):
    layers, rows, _ = dens_ref.shape
    small = [
        pltpu.make_async_copy(src, dst, small_sem.at[n])
        for n, (src, dst) in enumerate(
            ((occ_hbm, occ_ref), (transfer_hbm, transfer_ref), (absorb_hbm, absorb_ref))
        )
    ]
    loads = [pltpu.make_async_copy(dens_ref.at[n], raw.at[n], in_sem.at[n]) for n in range(layers)]
    stores = [pltpu.make_async_copy(packed.at[:, n], send_ref.at[:, n], out_sem.at[n]) for n in range(layers)]
    for copy in small[:1] + loads + small[1:]:
        copy.start()
    small[0].wait()
    occ = brick_mask(occ_ref)
    mask = jnp.concatenate(occ, axis=1)[None] > 0.5
    for layer in range(layers):
        loads[layer].wait()
        x = raw[layer].astype(F32)
        for s in range(S):
            for h in range(2):
                column = (2 * (S - 1 - s) + h) * H
                tmp[layer, h, pl.ds(s, rows, stride=S), :] = x[:, column : column + H]
        y = jnp.concatenate([tmp[layer, h].reshape(rows, S, H) for h in range(2)], axis=2)
        cells_ref[layer] = y.astype(BF16)
        sent = jnp.where(mask, y, -1.0).astype(BF16)
        for k in range(rows // 2):
            packed[light_slot(k, CELLS_FIRST), layer] = sent[2 * k : 2 * k + 2]
        stores[layer].start()
    for copy in small[1:]:
        copy.wait()
    for row in range(4):
        for n in range(4):
            const_ref[4 * row + n] = jnp.full((S, H), transfer_ref[row, n], F32)
    for c in range(3):
        const_ref[ABSORB + c] = jnp.full((S, H), absorb_ref[c] * (-1.0 / 32.0), F32)
    const_ref[PATH] = (2.0 / total_y) / jnp.abs(jnp.full((S, H), sign_ref[0], F32))
    for h in range(2):
        const_ref[OCCUPANCY + h] = occ[h]
    for store in stores:
        store.wait()


def propagate_kernel(recv_ref, rows_ref, const_ref, low_ref, high_ref, send_ref):
    del low_ref, high_ref
    blocks, layers = recv_ref.shape[0], recv_ref.shape[1]
    scale = [const_ref[ABSORB + c] for c in range(3)]

    def extinction(k):
        out = []
        for layer in range(layers):
            for d in halves(recv_ref[light_slot(k, CELLS_FIRST), layer].astype(F32)):
                out.append(jnp.where(d < 0.0, 0.0, softplus(polynomial(const_ref, 0, d))))
        return tuple(out)

    def emit(k, front):
        for c in range(3):
            send_ref[light_slot(k, FRONT_FIRST), c, :, :, :H] = front[2 * c].astype(BF16)
            send_ref[light_slot(k, FRONT_FIRST), c, :, :, H:] = front[2 * c + 1].astype(BF16)

    def block(k, carry):
        front, ext = list(carry[0]), carry[1]
        emit(k, front)
        for first in range(0, layers, 2):
            here, then = ext[2 * first : 2 * first + 2], ext[2 * first + 2 : 2 * first + 4]
            sides = [shifted(*then, 1, fill=1e30), then, shifted(*then, -1, fill=1e30)]
            for c in range(3):
                g = [f * jnp.exp(scale[c] * e) for f, e in zip(front[2 * c : 2 * c + 2], here)]
                g = [shifted(*g, 2), shifted(*g, 1), g, shifted(*g, -1), shifted(*g, -2)]
                lit = []
                for n in range(3):
                    arrived = tap(g[n], g[n + 1], g[n + 2])
                    lit.append([f * jnp.exp(scale[c] * e) for f, e in zip(arrived, sides[n])])
                front[2 * c : 2 * c + 2] = tap(*lit)
        return tuple(front), extinction(k + 1)

    init = tuple(x for c in range(3) for x in halves(rows_ref[c]))
    front, _ = lax.fori_loop(0, blocks - 1, block, (init, extinction(0)))
    emit(blocks - 1, front)


def local_kernel(
    cells_ref, light_ref, const_ref, sign_ref,
    ext_ref, gain_ref, slope_ref, base_ref, rows_ref, light, sem,
):
    layers, rows = cells_ref.shape[0], cells_ref.shape[1]
    load = pltpu.make_async_copy(light_ref, light, sem)
    load.start()
    occ = [const_ref[OCCUPANCY + h] for h in range(2)]
    back = sign_ref[0] < 0.0
    path = const_ref[PATH]

    def row(i, carry):
        r = jnp.where(back, rows - 1 - i, i)
        up = jnp.minimum(r + 1, rows - 1)
        down = jnp.maximum(r - 1, 0)
        column = [halves(cells_ref[layer, r].astype(F32)) for layer in range(layers)]
        new = []
        for layer in range(layers):
            through, base = carry[layer]
            d = column[layer]
            dn = halves(cells_ref[layer, up].astype(F32))
            dp = halves(cells_ref[layer, down].astype(F32))
            zp, zn = shifted(*d, 1), shifted(*d, -1)
            t_out, b_out = [], []
            for h in range(2):
                at = slice(h * H, (h + 1) * H)
                s = d[h]
                gy = 0.5 * (dn[h] - dp[h])
                gz = 0.5 * (zn[h] - zp[h])
                side, length = 0.36 * gy + 0.48 * gz, 1.0 + gy * gy + gz * gz
                if 0 < layer < layers - 1:
                    gx = 0.5 * (column[layer + 1][h] - column[layer - 1][h])
                    shading = 0.65 + 0.35 * ((0.8 * gx + side) * lax.rsqrt(length + gx * gx))
                else:
                    edge = 0 if layer == 0 else 1
                    slope_ref[edge, 0, r, :, at] = side
                    slope_ref[edge, 1, r, :, at] = length
                    shading = None
                ext = softplus(polynomial(const_ref, 0, s)) * occ[h]
                ext_ref[layer, r, :, at] = ext
                passing = jnp.exp(-ext * path)
                weight = through[h] * (1.0 - passing)
                colours = []
                for c in range(3):
                    lit = weight * jax.nn.sigmoid(polynomial(const_ref, c + 1, s))
                    colours.append(base[h][c] + lit)
                    gain_ref[layer, r, c, :, at] = lit if shading is None else lit * shading
                b_out.append(tuple(colours))
                t_out.append(through[h] * passing)
            new.append((tuple(t_out), tuple(b_out)))
        return tuple(new)

    one, zero = jnp.ones((S, H), F32), jnp.zeros((S, H), F32)
    init = tuple(((one, one), ((zero,) * 3, (zero,) * 3)) for _ in range(layers))
    final = lax.fori_loop(0, rows, row, init)
    for layer in range(layers):
        through, base = final[layer]
        for h in range(2):
            for c in range(3):
                base_ref[layer, c, :, h * H : (h + 1) * H] = 0.2 * base[h][c]
            base_ref[layer, 3, :, h * H : (h + 1) * H] = 1.0 - through[h]
    load.wait()
    start = 2 * lax.axis_index("light")
    for c in range(3):
        for r in range(2):
            for s in range(S):
                rows_ref[c, r, s : s + 1, :] = light[c, pl.ds(start + r, 1), (S - 1 - s) * T : (S - s) * T]


def place(send_ref, layer, h, c, value):
    start = (VIEW_FIRST - 16 * layer - h - 14) % 64
    split = min(S, (65 - start) // 2)
    send_ref[pl.ds(4 * start + c, split, stride=8), :] = value[:split]
    if split < S:
        send_ref[pl.ds(4 * (start + 2 * split - 64) + c, S - split, stride=8), :] = value[split:]


def shade_kernel(front_ref, low_ref, high_ref, cells_ref, ext_ref, gain_ref, slope_ref, base_ref, const_ref, send_ref, shade):
    layers, rows = ext_ref.shape[0], ext_ref.shape[1]

    def finish(i, carry):
        for r in (2 * i, 2 * i + 1):
            for edge in range(2):
                low = low_ref[r] if edge == 0 else cells_ref[layers - 2, r]
                high = cells_ref[1, r] if edge == 0 else high_ref[r]
                gx = 0.5 * (high.astype(F32) - low.astype(F32))
                facing = (0.8 * gx + slope_ref[edge, 0, r]) * lax.rsqrt(slope_ref[edge, 1, r] + gx * gx)
                shade[edge, r] = 0.65 + 0.35 * facing
        return carry

    lax.fori_loop(0, rows // 2, finish, 0)

    def channel(c, carry):
        scale = const_ref[ABSORB + c]
        front = [halves(front_ref[light_slot(r // 2, FRONT_FIRST), c, r % 2].astype(F32)) for r in range(rows)]
        for layer in range(layers):
            total = list(halves(base_ref[layer, c]))
            for r in range(rows):
                gain = halves(gain_ref[layer, r, c])
                if layer in (0, layers - 1):
                    gain = [g * s for g, s in zip(gain, halves(shade[min(layer, 1), r]))]
                total = [x + f * g for x, f, g in zip(total, front[r], gain)]
                if layer < layers - 1:
                    ext = halves(ext_ref[layer, r])
                    front[r] = blur(*[f * jnp.exp(scale * e) for f, e in zip(front[r], ext)])
            for h in range(2):
                place(send_ref, layer, h, c, total[h])
        return carry

    lax.fori_loop(0, 3, channel, 0)
    for layer in range(layers):
        for h in range(2):
            place(send_ref, layer, h, 3, base_ref[layer, 3, :, h * H : (h + 1) * H])


def merge_kernel(parts_ref, sign_ref, out_ref):
    back = sign_ref[0] >= 0.0
    late = 63 - VIEW_FIRST

    def over(near, far):
        through = 1.0 - near[3]
        return [near[c] + through * far[c] for c in range(4)]

    held = None
    for i in range(8):
        j = jnp.where(back, 7 - i, i)
        part = [parts_ref[pl.ds(4 * ((j - late) & 7) + c, 8, stride=32), :] for c in range(4)]
        if min(i, 7 - i) < late:
            part = [jnp.where(j < late, pltpu.roll(x, 1, 0), x) for x in part]
        held = part if held is None else over(held, part)
    for step in (1, 2, 4):
        other = [pltpu.roll(x, 8 - step, 0) for x in held]
        near = [jnp.where(back, o, h) for o, h in zip(other, held)]
        far = [jnp.where(back, h, o) for o, h in zip(other, held)]
        held = over(near, far)
    for c in range(4):
        out_ref[c : c + 1, :] = held[c][:1]


def in_vmem(x):
    return pltpu.with_memory_space_constraint(x, pltpu.VMEM)


def in_hbm(x):
    return pltpu.with_memory_space_constraint(x, pltpu.HBM)


def body(density, occupied, view_sign, transfer, absorb, light_in):
    layers, rows, columns = density.shape
    lights = lax.axis_size("light")
    views = lax.axis_size("view")
    out = pltpu.VMEM
    small = (occupied, transfer, absorb)

    cells, const, send = pl.pallas_call(
        lambda *refs: prepare_kernel(*refs, total_y=rows * views),
        out_shape=(
            out((layers, rows, S, T), BF16),
            out((PLANES, S, H), F32),
            pltpu.HBM((lights, layers, 2, S, T), BF16),
        ),
        in_specs=[ANY] * 4 + [SMEM],
        out_specs=(VMEM, VMEM, ANY),
        scratch_shapes=[
            pltpu.VMEM((layers, rows, columns), BF16),
            pltpu.VMEM((lights, layers, 2, S, T), BF16),
            pltpu.VMEM((layers, 2, rows * S, H), F32),
            *[pltpu.SMEM(x.shape, x.dtype) for x in small],
            pltpu.SemaphoreType.DMA((layers,)),
            pltpu.SemaphoreType.DMA((layers,)),
            pltpu.SemaphoreType.DMA((len(small),)),
        ],
        compiler_params=LIMIT,
        name="prepare",
    )(*[in_hbm(x) for x in (density, *small)], view_sign)
    const = in_vmem(const)

    cells_list, front_list = [
        [sorted(range(lights), key=lambda k: light_slot(k, first))] for first in (CELLS_FIRST, FRONT_FIRST)
    ]
    view_list = [[(VIEW_FIRST - k) % views for k in range(views)]]
    ends = lights - 1
    first, last = cells[0], cells[layers - 1]
    low = lax.ppermute(last, "light", [(i, i + 1) for i in range(ends)])
    high = lax.ppermute(first, "light", [(i + 1, i) for i in range(ends)])
    recv = lax.all_to_all(send, "light", 0, 0, axis_index_groups=cells_list)

    ext, gain, slope, base, light_rows = pl.pallas_call(
        local_kernel,
        out_shape=(
            out((layers, rows, S, T), F32),
            out((layers, rows, 3, S, T), F32),
            out((2, 2, rows, S, T), F32),
            out((layers, 4, S, T), F32),
            out((3, 2, S, T), F32),
        ),
        in_specs=[VMEM, ANY, VMEM, SMEM],
        out_specs=(VMEM,) * 5,
        scratch_shapes=[pltpu.VMEM(light_in.shape, F32), pltpu.SemaphoreType.DMA(())],
        compiler_params=LIMIT,
        name="local",
    )(in_vmem(cells), in_hbm(light_in), const, view_sign)

    fronts = pl.pallas_call(
        propagate_kernel,
        out_shape=out((lights, 3, 2, S, T), BF16),
        in_specs=[VMEM] * 5,
        out_specs=VMEM,
        compiler_params=LIMIT,
        name="propagate",
    )(in_vmem(recv), in_vmem(light_rows), const, in_vmem(low), in_vmem(high))
    front = lax.all_to_all(fronts, "light", 0, 0, axis_index_groups=front_list)

    partial = pl.pallas_call(
        shade_kernel,
        out_shape=out((views * 4, H), F32),
        in_specs=[VMEM] * 9,
        out_specs=VMEM,
        scratch_shapes=[pltpu.VMEM((2, rows, S, T), F32)],
        compiler_params=LIMIT,
        name="shade",
    )(*[in_vmem(x) for x in (front, low, high, cells, ext, gain, slope, base)], const)

    parts = lax.all_to_all(partial.reshape(views, 4, H), "view", 0, 0, axis_index_groups=view_list)
    parts = parts.reshape(views * 4, H)
    return pl.pallas_call(
        merge_kernel,
        out_shape=jax.ShapeDtypeStruct((4, H), F32),
        in_specs=[VMEM, SMEM],
        out_specs=VMEM,
        compiler_params=LIMIT,
        name="merge",
    )(in_vmem(parts), view_sign)


def solution(mesh):
    in_specs = (
        P("light", "view", None),
        P("light", "view", None),
        P(),
        P(),
        P(),
        P(None, "view", None),
    )
    out_specs = P(None, ("light", "view"))
    return jax.shard_map(body, mesh=mesh, in_specs=in_specs, out_specs=out_specs, check_vma=False)
```

```python
import jax
import jax.numpy as jnp
from jax import lax
from jax.experimental import pallas as pl
from jax.experimental.pallas import tpu as pltpu
from jax.sharding import PartitionSpec as P


S = 8
T = 256
H = 128
F32 = jnp.float32
BF16 = jnp.bfloat16
VMEM = pl.BlockSpec(memory_space=pltpu.VMEM)
ANY = pl.BlockSpec(memory_space=pl.ANY)
LIMIT = pltpu.CompilerParams(vmem_limit_bytes=16 << 20)
SMEM = pl.BlockSpec(memory_space=pltpu.SMEM)


CELLS_FIRST = 6
FRONT_FIRST = 4
VIEW_FIRST = 61


def light_slot(k, first):
    return (k - first) & 7


def halves(x):
    return x[..., :H], x[..., H:]


def shifted(a, b, by, fill=0.0):
    ra, rb = pltpu.roll(a, by % H, a.ndim - 1), pltpu.roll(b, by % H, a.ndim - 1)
    lane = lax.broadcasted_iota(jnp.int32, (S, H), 1)
    sub = lax.broadcasted_iota(jnp.int32, (S, H), 0)
    if by > 0:
        wrap = jnp.where(sub == S - 1, fill, pltpu.roll(rb, S - 1, a.ndim - 2))
        return jnp.where(lane < by, wrap, ra), jnp.where(lane < by, ra, rb)
    wrap = jnp.where(sub == 0, fill, pltpu.roll(ra, 1, a.ndim - 2))
    return jnp.where(lane >= H + by, rb, ra), jnp.where(lane >= H + by, wrap, rb)


def tap(before, cell, after):
    return [0.25 * (p + n) + 0.5 * c for p, c, n in zip(before, cell, after)]


def blur(a, b):
    return tap(shifted(a, b, 1), (a, b), shifted(a, b, -1))


ABSORB, PATH, OCCUPANCY, PLANES = 16, 19, 20, 22


def polynomial(const_ref, row, s):
    c = [const_ref[4 * row + n] for n in range(4)]
    return c[0] + s * (c[1] + s * (c[2] + s * c[3]))


def softplus(x):
    u = jnp.exp(-jnp.abs(x))
    tail = jnp.where(u < 2.0**-8, u * (1.0 - u * (0.5 - u * (1.0 / 3.0))), jnp.log(1.0 + u))
    return jnp.maximum(x, 0.0) + tail


def brick_mask(occ_ref):
    sub = lax.broadcasted_iota(jnp.int32, (S, H), 0)
    out = []
    for h in range(2):
        occ = jnp.zeros((S, H), F32)
        for s in range(S):
            occ = jnp.where(sub == s, occ_ref[0, 0, 2 * (S - 1 - s) + h].astype(F32), occ)
        out.append(occ)
    return out


def prepare_kernel(
    dens_ref, occ_hbm, transfer_hbm, absorb_hbm, sign_ref, cells_ref, const_ref, send_ref,
    raw, packed, tmp, occ_ref, transfer_ref, absorb_ref, in_sem, out_sem, small_sem, *, total_y,
):
    layers, rows, _ = dens_ref.shape
    small = [
        pltpu.make_async_copy(src, dst, small_sem.at[n])
        for n, (src, dst) in enumerate(
            ((occ_hbm, occ_ref), (transfer_hbm, transfer_ref), (absorb_hbm, absorb_ref))
        )
    ]
    loads = [pltpu.make_async_copy(dens_ref.at[n], raw.at[n], in_sem.at[n]) for n in range(layers)]
    stores = [pltpu.make_async_copy(packed.at[:, n], send_ref.at[:, n], out_sem.at[n]) for n in range(layers)]
    for copy in small[:1] + loads + small[1:]:
        copy.start()
    small[0].wait()
    occ = brick_mask(occ_ref)
    mask = jnp.concatenate(occ, axis=1)[None] > 0.5
    for layer in range(layers):
        loads[layer].wait()
        x = raw[layer].astype(F32)
        for s in range(S):
            for h in range(2):
                column = (2 * (S - 1 - s) + h) * H
                tmp[layer, h, pl.ds(s, rows, stride=S), :] = x[:, column : column + H]
        y = jnp.concatenate([tmp[layer, h].reshape(rows, S, H) for h in range(2)], axis=2)
        cells_ref[layer] = y.astype(BF16)
        sent = jnp.where(mask, y, -1.0).astype(BF16)
        for k in range(rows // 2):
            packed[light_slot(k, CELLS_FIRST), layer] = sent[2 * k : 2 * k + 2]
        stores[layer].start()
    for copy in small[1:]:
        copy.wait()
    for row in range(4):
        for n in range(4):
            const_ref[4 * row + n] = jnp.full((S, H), transfer_ref[row, n], F32)
    for c in range(3):
        const_ref[ABSORB + c] = jnp.full((S, H), absorb_ref[c] * (-1.0 / 32.0), F32)
    const_ref[PATH] = (2.0 / total_y) / jnp.abs(jnp.full((S, H), sign_ref[0], F32))
    for h in range(2):
        const_ref[OCCUPANCY + h] = occ[h]
    for store in stores:
        store.wait()


def propagate_kernel(recv_ref, rows_ref, const_ref, send_ref):
    blocks, layers = recv_ref.shape[0], recv_ref.shape[1]
    scale = [const_ref[ABSORB + c] for c in range(3)]

    def extinction(k):
        out = []
        for layer in range(layers):
            for d in halves(recv_ref[light_slot(k, CELLS_FIRST), layer].astype(F32)):
                out.append(jnp.where(d < 0.0, 0.0, softplus(polynomial(const_ref, 0, d))))
        return tuple(out)

    def emit(k, front):
        for c in range(3):
            send_ref[light_slot(k, FRONT_FIRST), c, :, :, :H] = front[2 * c].astype(BF16)
            send_ref[light_slot(k, FRONT_FIRST), c, :, :, H:] = front[2 * c + 1].astype(BF16)

    def block(k, carry):
        front, ext = list(carry[0]), carry[1]
        emit(k, front)
        for first in range(0, layers, 2):
            here, then = ext[2 * first : 2 * first + 2], ext[2 * first + 2 : 2 * first + 4]
            sides = [shifted(*then, 1, fill=1e30), then, shifted(*then, -1, fill=1e30)]
            for c in range(3):
                g = [f * jnp.exp(scale[c] * e) for f, e in zip(front[2 * c : 2 * c + 2], here)]
                g = [shifted(*g, 2), shifted(*g, 1), g, shifted(*g, -1), shifted(*g, -2)]
                lit = []
                for n in range(3):
                    arrived = tap(g[n], g[n + 1], g[n + 2])
                    lit.append([f * jnp.exp(scale[c] * e) for f, e in zip(arrived, sides[n])])
                front[2 * c : 2 * c + 2] = tap(*lit)
        return tuple(front), extinction(k + 1)

    init = tuple(x for c in range(3) for x in halves(rows_ref[c]))
    front, _ = lax.fori_loop(0, blocks - 1, block, (init, extinction(0)))
    emit(blocks - 1, front)


def local_kernel(
    cells_ref, light_ref, const_ref, sign_ref,
    ext_ref, gain_ref, slope_ref, base_ref, rows_ref, light, sem,
):
    layers, rows = cells_ref.shape[0], cells_ref.shape[1]
    load = pltpu.make_async_copy(light_ref, light, sem)
    load.start()
    occ = [const_ref[OCCUPANCY + h] for h in range(2)]
    back = sign_ref[0] < 0.0
    path = const_ref[PATH]

    def row(i, carry):
        r = jnp.where(back, rows - 1 - i, i)
        up = jnp.minimum(r + 1, rows - 1)
        down = jnp.maximum(r - 1, 0)
        column = [halves(cells_ref[layer, r].astype(F32)) for layer in range(layers)]
        new = []
        for layer in range(layers):
            through, base = carry[layer]
            d = column[layer]
            dn = halves(cells_ref[layer, up].astype(F32))
            dp = halves(cells_ref[layer, down].astype(F32))
            zp, zn = shifted(*d, 1), shifted(*d, -1)
            t_out, b_out = [], []
            for h in range(2):
                at = slice(h * H, (h + 1) * H)
                s = d[h]
                gy = 0.5 * (dn[h] - dp[h])
                gz = 0.5 * (zn[h] - zp[h])
                side, length = 0.36 * gy + 0.48 * gz, 1.0 + gy * gy + gz * gz
                if 0 < layer < layers - 1:
                    gx = 0.5 * (column[layer + 1][h] - column[layer - 1][h])
                    shading = 0.65 + 0.35 * ((0.8 * gx + side) * lax.rsqrt(length + gx * gx))
                else:
                    edge = 0 if layer == 0 else 1
                    slope_ref[edge, 0, r, :, at] = side
                    slope_ref[edge, 1, r, :, at] = length
                    shading = None
                ext = softplus(polynomial(const_ref, 0, s)) * occ[h]
                ext_ref[layer, r, :, at] = ext
                passing = jnp.exp(-ext * path)
                weight = through[h] * (1.0 - passing)
                colours = []
                for c in range(3):
                    lit = weight * jax.nn.sigmoid(polynomial(const_ref, c + 1, s))
                    colours.append(base[h][c] + lit)
                    gain_ref[layer, r, c, :, at] = lit if shading is None else lit * shading
                b_out.append(tuple(colours))
                t_out.append(through[h] * passing)
            new.append((tuple(t_out), tuple(b_out)))
        return tuple(new)

    one, zero = jnp.ones((S, H), F32), jnp.zeros((S, H), F32)
    init = tuple(((one, one), ((zero,) * 3, (zero,) * 3)) for _ in range(layers))
    final = lax.fori_loop(0, rows, row, init)
    for layer in range(layers):
        through, base = final[layer]
        for h in range(2):
            for c in range(3):
                base_ref[layer, c, :, h * H : (h + 1) * H] = 0.2 * base[h][c]
            base_ref[layer, 3, :, h * H : (h + 1) * H] = 1.0 - through[h]
    load.wait()
    start = 2 * lax.axis_index("light")
    for c in range(3):
        for r in range(2):
            for s in range(S):
                rows_ref[c, r, s : s + 1, :] = light[c, pl.ds(start + r, 1), (S - 1 - s) * T : (S - s) * T]


def place(send_ref, layer, h, c, value):
    start = (VIEW_FIRST - 16 * layer - h - 14) % 64
    split = min(S, (65 - start) // 2)
    send_ref[pl.ds(4 * start + c, split, stride=8), :] = value[:split]
    if split < S:
        send_ref[pl.ds(4 * (start + 2 * split - 64) + c, S - split, stride=8), :] = value[split:]


def shade_kernel(front_ref, low_ref, high_ref, cells_ref, ext_ref, gain_ref, slope_ref, base_ref, const_ref, send_ref, shade):
    layers, rows = ext_ref.shape[0], ext_ref.shape[1]

    def finish(i, carry):
        for r in (2 * i, 2 * i + 1):
            for edge in range(2):
                low = low_ref[r] if edge == 0 else cells_ref[layers - 2, r]
                high = cells_ref[1, r] if edge == 0 else high_ref[r]
                gx = 0.5 * (high.astype(F32) - low.astype(F32))
                facing = (0.8 * gx + slope_ref[edge, 0, r]) * lax.rsqrt(slope_ref[edge, 1, r] + gx * gx)
                shade[edge, r] = 0.65 + 0.35 * facing
        return carry

    lax.fori_loop(0, rows // 2, finish, 0)

    def channel(c, carry):
        scale = const_ref[ABSORB + c]
        front = [halves(front_ref[light_slot(r // 2, FRONT_FIRST), c, r % 2].astype(F32)) for r in range(rows)]
        for layer in range(layers):
            total = list(halves(base_ref[layer, c]))
            for r in range(rows):
                gain = halves(gain_ref[layer, r, c])
                if layer in (0, layers - 1):
                    gain = [g * s for g, s in zip(gain, halves(shade[min(layer, 1), r]))]
                total = [x + f * g for x, f, g in zip(total, front[r], gain)]
                if layer < layers - 1:
                    ext = halves(ext_ref[layer, r])
                    front[r] = blur(*[f * jnp.exp(scale * e) for f, e in zip(front[r], ext)])
            for h in range(2):
                place(send_ref, layer, h, c, total[h])
        return carry

    lax.fori_loop(0, 3, channel, 0)
    for layer in range(layers):
        for h in range(2):
            place(send_ref, layer, h, 3, base_ref[layer, 3, :, h * H : (h + 1) * H])


def merge_kernel(parts_ref, sign_ref, out_ref):
    back = sign_ref[0] >= 0.0
    late = 63 - VIEW_FIRST

    def over(near, far):
        through = 1.0 - near[3]
        return [near[c] + through * far[c] for c in range(4)]

    held = None
    for i in range(8):
        j = jnp.where(back, 7 - i, i)
        part = [parts_ref[pl.ds(4 * ((j - late) & 7) + c, 8, stride=32), :] for c in range(4)]
        if min(i, 7 - i) < late:
            part = [jnp.where(j < late, pltpu.roll(x, 1, 0), x) for x in part]
        held = part if held is None else over(held, part)
    for step in (1, 2, 4):
        other = [pltpu.roll(x, 8 - step, 0) for x in held]
        near = [jnp.where(back, o, h) for o, h in zip(other, held)]
        far = [jnp.where(back, h, o) for o, h in zip(other, held)]
        held = over(near, far)
    for c in range(4):
        out_ref[c : c + 1, :] = held[c][:1]


def in_vmem(x):
    return pltpu.with_memory_space_constraint(x, pltpu.VMEM)


def in_hbm(x):
    return pltpu.with_memory_space_constraint(x, pltpu.HBM)


def body(density, occupied, view_sign, transfer, absorb, light_in):
    layers, rows, columns = density.shape
    lights = lax.axis_size("light")
    views = lax.axis_size("view")
    out = pltpu.VMEM
    small = (occupied, transfer, absorb)

    cells, const, send = pl.pallas_call(
        lambda *refs: prepare_kernel(*refs, total_y=rows * views),
        out_shape=(
            out((layers, rows, S, T), BF16),
            out((PLANES, S, H), F32),
            pltpu.HBM((lights, layers, 2, S, T), BF16),
        ),
        in_specs=[ANY] * 4 + [SMEM],
        out_specs=(VMEM, VMEM, ANY),
        scratch_shapes=[
            pltpu.VMEM((layers, rows, columns), BF16),
            pltpu.VMEM((lights, layers, 2, S, T), BF16),
            pltpu.VMEM((layers, 2, rows * S, H), F32),
            *[pltpu.SMEM(x.shape, x.dtype) for x in small],
            pltpu.SemaphoreType.DMA((layers,)),
            pltpu.SemaphoreType.DMA((layers,)),
            pltpu.SemaphoreType.DMA((len(small),)),
        ],
        compiler_params=LIMIT,
        name="prepare",
    )(*[in_hbm(x) for x in (density, *small)], view_sign)
    const = in_vmem(const)

    cells_list, front_list = [
        [sorted(range(lights), key=lambda k: light_slot(k, first))] for first in (CELLS_FIRST, FRONT_FIRST)
    ]
    view_list = [[(VIEW_FIRST - k) % views for k in range(views)]]
    ends = lights - 1
    first, last = cells[0], cells[layers - 1]
    low = lax.ppermute(last, "light", [(i, i + 1) for i in range(ends)])
    high = lax.ppermute(first, "light", [(i + 1, i) for i in range(ends)])
    recv = lax.all_to_all(send, "light", 0, 0, axis_index_groups=cells_list)

    ext, gain, slope, base, light_rows = pl.pallas_call(
        local_kernel,
        out_shape=(
            out((layers, rows, S, T), F32),
            out((layers, rows, 3, S, T), F32),
            out((2, 2, rows, S, T), F32),
            out((layers, 4, S, T), F32),
            out((3, 2, S, T), F32),
        ),
        in_specs=[VMEM, ANY, VMEM, SMEM],
        out_specs=(VMEM,) * 5,
        scratch_shapes=[pltpu.VMEM(light_in.shape, F32), pltpu.SemaphoreType.DMA(())],
        compiler_params=LIMIT,
        name="local",
    )(in_vmem(cells), in_hbm(light_in), const, view_sign)

    propagate = pl.pallas_call(
        propagate_kernel,
        out_shape=out((lights, 3, 2, S, T), BF16),
        in_specs=[VMEM] * 3,
        out_specs=VMEM,
        compiler_params=LIMIT,
        name="propagate",
    )
    fronts = propagate(in_vmem(recv), in_vmem(light_rows), const)
    fronts, low, high = lax.optimization_barrier((fronts, low, high))
    front = lax.all_to_all(fronts, "light", 0, 0, axis_index_groups=front_list)

    partial = pl.pallas_call(
        shade_kernel,
        out_shape=out((views * 4, H), F32),
        in_specs=[VMEM] * 9,
        out_specs=VMEM,
        scratch_shapes=[pltpu.VMEM((2, rows, S, T), F32)],
        compiler_params=LIMIT,
        name="shade",
    )(*[in_vmem(x) for x in (front, low, high, cells, ext, gain, slope, base)], const)

    parts = lax.all_to_all(partial.reshape(views, 4, H), "view", 0, 0, axis_index_groups=view_list)
    parts = parts.reshape(views * 4, H)
    return pl.pallas_call(
        merge_kernel,
        out_shape=jax.ShapeDtypeStruct((4, H), F32),
        in_specs=[VMEM, SMEM],
        out_specs=VMEM,
        compiler_params=LIMIT,
        name="merge",
    )(in_vmem(parts), view_sign)


def solution(mesh):
    in_specs = (
        P("light", "view", None),
        P("light", "view", None),
        P(),
        P(),
        P(),
        P(None, "view", None),
    )
    out_specs = P(None, ("light", "view"))
    return jax.shard_map(body, mesh=mesh, in_specs=in_specs, out_specs=out_specs, check_vma=False)
```

```python
import jax
import jax.numpy as jnp
from jax import lax
from jax.experimental import pallas as pl
from jax.experimental.pallas import tpu as pltpu
from jax.sharding import PartitionSpec as P


S = 8
T = 256
H = 128
F32 = jnp.float32
BF16 = jnp.bfloat16
VMEM = pl.BlockSpec(memory_space=pltpu.VMEM)
ANY = pl.BlockSpec(memory_space=pl.ANY)
LIMIT = pltpu.CompilerParams(vmem_limit_bytes=16 << 20)
SMEM = pl.BlockSpec(memory_space=pltpu.SMEM)


CELLS_FIRST = 6
FRONT_FIRST = 4
VIEW_FIRST = 61


def light_slot(k, first):
    return (k - first) & 7


def halves(x):
    return x[..., :H], x[..., H:]


def shifted(a, b, by, fill=0.0):
    ra, rb = pltpu.roll(a, by % H, a.ndim - 1), pltpu.roll(b, by % H, a.ndim - 1)
    lane = lax.broadcasted_iota(jnp.int32, (S, H), 1)
    sub = lax.broadcasted_iota(jnp.int32, (S, H), 0)
    if by > 0:
        wrap = jnp.where(sub == S - 1, fill, pltpu.roll(rb, S - 1, a.ndim - 2))
        return jnp.where(lane < by, wrap, ra), jnp.where(lane < by, ra, rb)
    wrap = jnp.where(sub == 0, fill, pltpu.roll(ra, 1, a.ndim - 2))
    return jnp.where(lane >= H + by, rb, ra), jnp.where(lane >= H + by, wrap, rb)


def tap(before, cell, after):
    return [0.25 * (p + n) + 0.5 * c for p, c, n in zip(before, cell, after)]


def blur(a, b):
    return tap(shifted(a, b, 1), (a, b), shifted(a, b, -1))


ABSORB, PATH, OCCUPANCY, PLANES = 16, 19, 20, 22


def polynomial(const_ref, row, s):
    c = [const_ref[4 * row + n] for n in range(4)]
    return c[0] + s * (c[1] + s * (c[2] + s * c[3]))


def softplus(x):
    u = jnp.exp(-jnp.abs(x))
    tail = jnp.where(u < 2.0**-8, u * (1.0 - u * (0.5 - u * (1.0 / 3.0))), jnp.log(1.0 + u))
    return jnp.maximum(x, 0.0) + tail


def brick_mask(occ_ref):
    sub = lax.broadcasted_iota(jnp.int32, (S, H), 0)
    out = []
    for h in range(2):
        occ = jnp.zeros((S, H), F32)
        for s in range(S):
            occ = jnp.where(sub == s, occ_ref[0, 0, 2 * (S - 1 - s) + h].astype(F32), occ)
        out.append(occ)
    return out


def prepare_kernel(
    dens_ref, occ_hbm, transfer_hbm, absorb_hbm, light_hbm, sign_ref, cells_ref, const_ref, rows_ref, send_ref,
    raw, packed, light, tmp, occ_ref, transfer_ref, absorb_ref, in_sem, out_sem, small_sem, light_sem, *, total_y,
):
    layers, rows, _ = dens_ref.shape
    small = [
        pltpu.make_async_copy(src, dst, small_sem.at[n])
        for n, (src, dst) in enumerate(
            ((occ_hbm, occ_ref), (transfer_hbm, transfer_ref), (absorb_hbm, absorb_ref))
        )
    ]
    loads = [pltpu.make_async_copy(dens_ref.at[n], raw.at[n], in_sem.at[n]) for n in range(layers)]
    stores = [pltpu.make_async_copy(packed.at[:, n], send_ref.at[:, n], out_sem.at[n]) for n in range(layers)]
    light_load = pltpu.make_async_copy(light_hbm, light, light_sem)
    for copy in small[:1] + loads + small[1:] + [light_load]:
        copy.start()
    small[0].wait()
    occ = brick_mask(occ_ref)
    mask = jnp.concatenate(occ, axis=1)[None] > 0.5
    for layer in range(layers):
        loads[layer].wait()
        x = raw[layer].astype(F32)
        for s in range(S):
            for h in range(2):
                column = (2 * (S - 1 - s) + h) * H
                tmp[layer, h, pl.ds(s, rows, stride=S), :] = x[:, column : column + H]
        y = jnp.concatenate([tmp[layer, h].reshape(rows, S, H) for h in range(2)], axis=2)
        cells_ref[layer] = y.astype(BF16)
        sent = jnp.where(mask, y, -1.0).astype(BF16)
        for k in range(rows // 2):
            packed[light_slot(k, CELLS_FIRST), layer] = sent[2 * k : 2 * k + 2]
        stores[layer].start()
    for copy in small[1:]:
        copy.wait()
    for row in range(4):
        for n in range(4):
            const_ref[4 * row + n] = jnp.full((S, H), transfer_ref[row, n], F32)
    for c in range(3):
        const_ref[ABSORB + c] = jnp.full((S, H), absorb_ref[c] * (-1.0 / 32.0), F32)
    const_ref[PATH] = (2.0 / total_y) / jnp.abs(jnp.full((S, H), sign_ref[0], F32))
    for h in range(2):
        const_ref[OCCUPANCY + h] = occ[h]
    light_load.wait()
    start = 2 * lax.axis_index("light")
    for c in range(3):
        for r in range(2):
            for s in range(S):
                rows_ref[c, r, s : s + 1, :] = light[c, pl.ds(start + r, 1), (S - 1 - s) * T : (S - s) * T]
    for store in stores:
        store.wait()


def propagate_kernel(recv_ref, rows_ref, const_ref, send_ref):
    blocks, layers = recv_ref.shape[0], recv_ref.shape[1]
    scale = [const_ref[ABSORB + c] for c in range(3)]

    def extinction(k):
        out = []
        for layer in range(layers):
            for d in halves(recv_ref[light_slot(k, CELLS_FIRST), layer].astype(F32)):
                out.append(jnp.where(d < 0.0, 0.0, softplus(polynomial(const_ref, 0, d))))
        return tuple(out)

    def emit(k, front):
        for c in range(3):
            send_ref[light_slot(k, FRONT_FIRST), c, :, :, :H] = front[2 * c].astype(BF16)
            send_ref[light_slot(k, FRONT_FIRST), c, :, :, H:] = front[2 * c + 1].astype(BF16)

    def block(k, carry):
        front, ext = list(carry[0]), carry[1]
        emit(k, front)
        for first in range(0, layers, 2):
            here, then = ext[2 * first : 2 * first + 2], ext[2 * first + 2 : 2 * first + 4]
            sides = [shifted(*then, 1, fill=1e30), then, shifted(*then, -1, fill=1e30)]
            for c in range(3):
                g = [f * jnp.exp(scale[c] * e) for f, e in zip(front[2 * c : 2 * c + 2], here)]
                g = [shifted(*g, 2), shifted(*g, 1), g, shifted(*g, -1), shifted(*g, -2)]
                lit = []
                for n in range(3):
                    arrived = tap(g[n], g[n + 1], g[n + 2])
                    lit.append([f * jnp.exp(scale[c] * e) for f, e in zip(arrived, sides[n])])
                front[2 * c : 2 * c + 2] = tap(*lit)
        return tuple(front), extinction(k + 1)

    init = tuple(x for c in range(3) for x in halves(rows_ref[c]))
    front, _ = lax.fori_loop(0, blocks - 1, block, (init, extinction(0)))
    emit(blocks - 1, front)


def local_kernel(
    cells_ref, const_ref, sign_ref,
    ext_ref, gain_ref, slope_ref, base_ref,
):
    layers, rows = cells_ref.shape[0], cells_ref.shape[1]
    occ = [const_ref[OCCUPANCY + h] for h in range(2)]
    back = sign_ref[0] < 0.0
    path = const_ref[PATH]

    def row(i, carry):
        r = jnp.where(back, rows - 1 - i, i)
        up = jnp.minimum(r + 1, rows - 1)
        down = jnp.maximum(r - 1, 0)
        column = [halves(cells_ref[layer, r].astype(F32)) for layer in range(layers)]
        new = []
        for layer in range(layers):
            through, base = carry[layer]
            d = column[layer]
            dn = halves(cells_ref[layer, up].astype(F32))
            dp = halves(cells_ref[layer, down].astype(F32))
            zp, zn = shifted(*d, 1), shifted(*d, -1)
            t_out, b_out = [], []
            for h in range(2):
                at = slice(h * H, (h + 1) * H)
                s = d[h]
                gy = 0.5 * (dn[h] - dp[h])
                gz = 0.5 * (zn[h] - zp[h])
                side, length = 0.36 * gy + 0.48 * gz, 1.0 + gy * gy + gz * gz
                if 0 < layer < layers - 1:
                    gx = 0.5 * (column[layer + 1][h] - column[layer - 1][h])
                    shading = 0.65 + 0.35 * ((0.8 * gx + side) * lax.rsqrt(length + gx * gx))
                else:
                    edge = 0 if layer == 0 else 1
                    slope_ref[edge, 0, r, :, at] = side
                    slope_ref[edge, 1, r, :, at] = length
                    shading = None
                ext = softplus(polynomial(const_ref, 0, s)) * occ[h]
                ext_ref[layer, r, :, at] = ext
                passing = jnp.exp(-ext * path)
                weight = through[h] * (1.0 - passing)
                colours = []
                for c in range(3):
                    lit = weight * jax.nn.sigmoid(polynomial(const_ref, c + 1, s))
                    colours.append(base[h][c] + lit)
                    gain_ref[layer, r, c, :, at] = lit if shading is None else lit * shading
                b_out.append(tuple(colours))
                t_out.append(through[h] * passing)
            new.append((tuple(t_out), tuple(b_out)))
        return tuple(new)

    one, zero = jnp.ones((S, H), F32), jnp.zeros((S, H), F32)
    init = tuple(((one, one), ((zero,) * 3, (zero,) * 3)) for _ in range(layers))
    final = lax.fori_loop(0, rows, row, init)
    for layer in range(layers):
        through, base = final[layer]
        for h in range(2):
            for c in range(3):
                base_ref[layer, c, :, h * H : (h + 1) * H] = 0.2 * base[h][c]
            base_ref[layer, 3, :, h * H : (h + 1) * H] = 1.0 - through[h]


def place(send_ref, layer, h, c, value):
    start = (VIEW_FIRST - 16 * layer - h - 14) % 64
    split = min(S, (65 - start) // 2)
    send_ref[pl.ds(4 * start + c, split, stride=8), :] = value[:split]
    if split < S:
        send_ref[pl.ds(4 * (start + 2 * split - 64) + c, S - split, stride=8), :] = value[split:]


def shade_kernel(front_ref, low_ref, high_ref, cells_ref, ext_ref, gain_ref, slope_ref, base_ref, const_ref, send_ref, shade):
    layers, rows = ext_ref.shape[0], ext_ref.shape[1]

    def finish(i, carry):
        for r in (2 * i, 2 * i + 1):
            for edge in range(2):
                low = low_ref[r] if edge == 0 else cells_ref[layers - 2, r]
                high = cells_ref[1, r] if edge == 0 else high_ref[r]
                gx = 0.5 * (high.astype(F32) - low.astype(F32))
                facing = (0.8 * gx + slope_ref[edge, 0, r]) * lax.rsqrt(slope_ref[edge, 1, r] + gx * gx)
                shade[edge, r] = 0.65 + 0.35 * facing
        return carry

    lax.fori_loop(0, rows // 2, finish, 0)

    def channel(c, carry):
        scale = const_ref[ABSORB + c]
        front = [halves(front_ref[light_slot(r // 2, FRONT_FIRST), c, r % 2].astype(F32)) for r in range(rows)]
        for layer in range(layers):
            total = list(halves(base_ref[layer, c]))
            for r in range(rows):
                gain = halves(gain_ref[layer, r, c])
                if layer in (0, layers - 1):
                    gain = [g * s for g, s in zip(gain, halves(shade[min(layer, 1), r]))]
                total = [x + f * g for x, f, g in zip(total, front[r], gain)]
                if layer < layers - 1:
                    ext = halves(ext_ref[layer, r])
                    front[r] = blur(*[f * jnp.exp(scale * e) for f, e in zip(front[r], ext)])
            for h in range(2):
                place(send_ref, layer, h, c, total[h])
        return carry

    lax.fori_loop(0, 3, channel, 0)
    for layer in range(layers):
        for h in range(2):
            place(send_ref, layer, h, 3, base_ref[layer, 3, :, h * H : (h + 1) * H])


def merge_kernel(parts_ref, sign_ref, out_ref):
    back = sign_ref[0] >= 0.0
    late = 63 - VIEW_FIRST

    def over(near, far):
        through = 1.0 - near[3]
        return [near[c] + through * far[c] for c in range(4)]

    held = None
    for i in range(8):
        j = jnp.where(back, 7 - i, i)
        part = [parts_ref[pl.ds(4 * ((j - late) & 7) + c, 8, stride=32), :] for c in range(4)]
        if min(i, 7 - i) < late:
            part = [jnp.where(j < late, pltpu.roll(x, 1, 0), x) for x in part]
        held = part if held is None else over(held, part)
    for step in (1, 2, 4):
        other = [pltpu.roll(x, 8 - step, 0) for x in held]
        near = [jnp.where(back, o, h) for o, h in zip(other, held)]
        far = [jnp.where(back, h, o) for o, h in zip(other, held)]
        held = over(near, far)
    for c in range(4):
        out_ref[c : c + 1, :] = held[c][:1]


def in_vmem(x):
    return pltpu.with_memory_space_constraint(x, pltpu.VMEM)


def in_hbm(x):
    return pltpu.with_memory_space_constraint(x, pltpu.HBM)


def body(density, occupied, view_sign, transfer, absorb, light_in):
    layers, rows, columns = density.shape
    lights = lax.axis_size("light")
    views = lax.axis_size("view")
    out = pltpu.VMEM
    small = (occupied, transfer, absorb)

    cells, const, light_rows, send = pl.pallas_call(
        lambda *refs: prepare_kernel(*refs, total_y=rows * views),
        out_shape=(
            out((layers, rows, S, T), BF16),
            out((PLANES, S, H), F32),
            out((3, 2, S, T), F32),
            pltpu.HBM((lights, layers, 2, S, T), BF16),
        ),
        in_specs=[ANY] * 5 + [SMEM],
        out_specs=(VMEM, VMEM, VMEM, ANY),
        scratch_shapes=[
            pltpu.VMEM((layers, rows, columns), BF16),
            pltpu.VMEM((lights, layers, 2, S, T), BF16),
            pltpu.VMEM(light_in.shape, F32),
            pltpu.VMEM((layers, 2, rows * S, H), F32),
            *[pltpu.SMEM(x.shape, x.dtype) for x in small],
            pltpu.SemaphoreType.DMA((layers,)),
            pltpu.SemaphoreType.DMA((layers,)),
            pltpu.SemaphoreType.DMA((len(small),)),
            pltpu.SemaphoreType.DMA(()),
        ],
        compiler_params=LIMIT,
        name="prepare",
    )(*[in_hbm(x) for x in (density, *small, light_in)], view_sign)
    const = in_vmem(const)

    cells_list, front_list = [
        [sorted(range(lights), key=lambda k: light_slot(k, first))] for first in (CELLS_FIRST, FRONT_FIRST)
    ]
    view_list = [[(VIEW_FIRST - k) % views for k in range(views)]]
    ends = lights - 1
    first, last = cells[0], cells[layers - 1]
    low = lax.ppermute(last, "light", [(i, i + 1) for i in range(ends)])
    high = lax.ppermute(first, "light", [(i + 1, i) for i in range(ends)])
    recv = lax.all_to_all(send, "light", 0, 0, axis_index_groups=cells_list)

    ext, gain, slope, base = pl.pallas_call(
        local_kernel,
        out_shape=(
            out((layers, rows, S, T), F32),
            out((layers, rows, 3, S, T), F32),
            out((2, 2, rows, S, T), F32),
            out((layers, 4, S, T), F32),
        ),
        in_specs=[VMEM, VMEM, SMEM],
        out_specs=(VMEM,) * 4,
        compiler_params=LIMIT,
        name="local",
    )(in_vmem(cells), const, view_sign)

    propagate = pl.pallas_call(
        propagate_kernel,
        out_shape=out((lights, 3, 2, S, T), BF16),
        in_specs=[VMEM] * 3,
        out_specs=VMEM,
        compiler_params=LIMIT,
        name="propagate",
    )
    fronts = propagate(in_vmem(recv), in_vmem(light_rows), const)
    fronts, low, high = lax.optimization_barrier((fronts, low, high))
    front = lax.all_to_all(fronts, "light", 0, 0, axis_index_groups=front_list)

    partial = pl.pallas_call(
        shade_kernel,
        out_shape=out((views * 4, H), F32),
        in_specs=[VMEM] * 9,
        out_specs=VMEM,
        scratch_shapes=[pltpu.VMEM((2, rows, S, T), F32)],
        compiler_params=LIMIT,
        name="shade",
    )(*[in_vmem(x) for x in (front, low, high, cells, ext, gain, slope, base)], const)

    parts = lax.all_to_all(partial.reshape(views, 4, H), "view", 0, 0, axis_index_groups=view_list)
    parts = parts.reshape(views * 4, H)
    return pl.pallas_call(
        merge_kernel,
        out_shape=jax.ShapeDtypeStruct((4, H), F32),
        in_specs=[VMEM, SMEM],
        out_specs=VMEM,
        compiler_params=LIMIT,
        name="merge",
    )(in_vmem(parts), view_sign)


def solution(mesh):
    in_specs = (
        P("light", "view", None),
        P("light", "view", None),
        P(),
        P(),
        P(),
        P(None, "view", None),
    )
    out_specs = P(None, ("light", "view"))
    return jax.shard_map(body, mesh=mesh, in_specs=in_specs, out_specs=out_specs, check_vma=False)
```
